128 devices in a mesh: bx: 4 (over y), by: 4 (over x), bz: 8 (over z, core).
Axes of the slice: x: 4, y: 4, z: 4, core: 2. Of those that a mesh axis runs over, the one named last changes fastest.
Arguments:
- position: float32 [3, 128, 128, 2048], P(None, 'bx', 'by', 'bz'), may hold values from -2 to 2
- velocity: float32 [3, 128, 128, 2048], P(None, 'bx', 'by', 'bz'), may hold values from -3 to 3
- density: float32 [128, 128, 2048], P('bx', 'by', 'bz'), may hold values from 0.5 to 2
- energy: float32 [128, 128, 2048], P('bx', 'by', 'bz'), may hold values from 0.1 to 10
- pinned: int32 [128, 128, 2048], P('bx', 'by', 'bz'), may hold values 0 or 1
Outputs:
- velocity_new: float32 [3, 128, 128, 2048], P(None, 'bx', 'by', 'bz')
- accel: float32 [3, 128, 128, 2048], P(None, 'bx', 'by', 'bz')
- relaxed: float32 [3, 128, 128, 2048], P(None, 'bx', 'by', 'bz')
- density_new: float32 [128, 128, 2048], P('bx', 'by', 'bz')
- energy_new: float32 [128, 128, 2048], P('bx', 'by', 'bz')
The draws below stay inside these ranges and needn't reach their ends.
All inputs are finite; a program needn't handle non-finite values. No bound on the sum of `pinned` on one device may be relied on, other than what follows from the above.
Results may differ from the reference program's by a relative error of at most 0.0003.
Values sent between devices are 32-bit elements; how exact they have to be, the bound alone decides.
A program may use at most 128 MiB of HBM per device.

```python
import math
import jax
import jax.numpy as jnp

CG_ITERS = 2
SWEEPS = 3
NX = 128
NY = 128
NZ = 2048


def plant(drawn, key, least, top_value):
    shape = drawn.shape
    index_at = [jax.random.randint(jax.random.fold_in(key, axis), (), 0, shape[axis]) for axis in range(len(shape))]
    drawn = drawn.at[tuple(index_at)].set(least)
    longest = shape.index(max(shape))
    index_at[longest] = (index_at[longest] + 1) % shape[longest]
    return drawn.at[tuple(index_at)].set(top_value)


def block_scale(key, extent, shards, least, largest):
    loudness = 1.0
    for axis_at, blocks in shards:
        draws = jax.random.uniform(jax.random.fold_in(jax.random.fold_in(key, 6), axis_at), (blocks,), jnp.float32, least / len(shards), largest / len(shards))
        loudness = loudness * jnp.repeat(jnp.exp(draws), extent[axis_at] // blocks).reshape((-1,) + (1,) * (len(extent) - 1 - axis_at))
    return loudness


def bell_draw(rng, dims, scale, most, shards=(), kind=jnp.bfloat16):
    values = jax.random.normal(rng, dims, jnp.float32) * scale
    if len(shards) > 0:
        values = block_scale(rng, dims, shards, -0.22, 0.18) * values
    return jnp.clip(values, min=-most, max=most).astype(kind)


def setup_inputs(seed: int = 0) -> dict:
    streams_of = jax.random.split(jax.random.key(seed), 6)
    return {
        "position": bell_draw(streams_of[0], (3, NX, NY, NZ), 0.3, 2.0, ((1, 4), (2, 4), (3, 8)), jnp.float32),
        "velocity": bell_draw(streams_of[1], (3, NX, NY, NZ), 0.4, 3.0, ((1, 4), (2, 4), (3, 8)), jnp.float32),
        "density": jnp.clip(0.5 + 1.5 * jax.random.uniform(streams_of[2], (NX, NY, NZ), jnp.float32) ** block_scale(streams_of[2], (NX, NY, NZ), ((0, 4), (1, 4), (2, 8)), -0.2, 0.2), 0.5, 2.0),
        "energy": jnp.clip(jnp.exp(math.log(10.0) - 4.6051702 * jax.random.uniform(streams_of[3], (NX, NY, NZ), jnp.float32) ** block_scale(streams_of[3], (NX, NY, NZ), ((0, 4), (1, 4), (2, 8)), -0.2, 0.2)), 0.1, 10.0),
        "pinned": plant((jax.random.randint(streams_of[4], (NX, NY, NZ), 0, 8) < 1).astype(jnp.int32), jax.random.fold_in(streams_of[4], 1), 0, 1),
    }


TIME_STEP = 0.6
RELAX_RATE = 0.8
CONSISTENT = 0.2


def pad_cells(values):
    return jnp.pad(values, [(0, 0)] * (values.ndim - 3) + [(1, 1)] * 3)


def shift_triple(along_dim, along, first, second):
    offsets = [0, 0, 0]
    offsets[along_dim] = along
    others = [d for d in range(3) if d != along_dim]
    offsets[others[0]] = first
    offsets[others[1]] = second
    return offsets


def select_at(extended, offsets):
    sizes = extended.shape[-3:]
    return extended[..., 1 + offsets[0]:sizes[0] - 1 + offsets[0], 1 + offsets[1]:sizes[1] - 1 + offsets[1], 1 + offsets[2]:sizes[2] - 1 + offsets[2]]


def corner_force(pressure_ext):
    parts = []
    for along_dim in range(3):
        summed = 0.0
        for first in (0, -1):
            for second in (0, -1):
                summed = summed + select_at(pressure_ext, shift_triple(along_dim, -1, first, second)) - select_at(pressure_ext, shift_triple(along_dim, 0, first, second))
        parts.append(0.25 * summed)
    return jnp.stack(parts)


def node_mass(density_ext):
    summed = 0.0
    for first in (0, -1):
        for second in (0, -1):
            for third in (0, -1):
                summed = summed + select_at(density_ext, [first, second, third])
    return 0.125 * summed


def neighbours(extended):
    summed = 0.0
    for along_dim in range(3):
        for along in (-1, 1):
            summed = summed + select_at(extended, shift_triple(along_dim, along, 0, 0))
    return summed


def mass_apply(vector, extended, masses):
    return masses * vector + CONSISTENT * (6.0 * vector + neighbours(extended))


def divergence(vel_ext):
    summed = 0.0
    for along_dim in range(3):
        for first in (0, 1):
            for second in (0, 1):
                summed = summed + select_at(vel_ext[along_dim], shift_triple(along_dim, 1, first, second)) - select_at(vel_ext[along_dim], shift_triple(along_dim, 0, first, second))
    return 0.25 * summed


def face_flux(packed, along_dim, along):
    speed = 0.0
    for first in (0, 1):
        for second in (0, 1):
            speed = speed + select_at(packed[along_dim], shift_triple(along_dim, along, first, second))
    speed = 0.25 * speed
    upper = select_at(packed[3:5], shift_triple(along_dim, along, 0, 0))
    lower = select_at(packed[3:5], shift_triple(along_dim, along - 1, 0, 0))
    return speed * jnp.where(speed > 0, upper, lower)


def remap_cells(packed):
    result = select_at(packed[3:5], [0, 0, 0])
    for along_dim in range(3):
        result = result + face_flux(packed, along_dim, 1) - face_flux(packed, along_dim, 0)
    return result


def inner(first, second):
    return jnp.sum(first * second, axis=(1, 2, 3), keepdims=True)


def reference(position, velocity, density, energy, pinned):
    cells = pad_cells(jnp.stack([density, energy]))
    force = corner_force(0.4 * cells[0] * cells[1])
    masses = node_mass(cells[0])
    solution = jnp.zeros_like(force)
    residual = force
    direction = force
    norm_now = inner(residual, residual)
    for step_index in range(CG_ITERS):
        image = mass_apply(direction, pad_cells(direction), masses)
        alpha = norm_now / inner(direction, image)
        solution = solution + alpha * direction
        residual = residual - alpha * image
        norm_next = inner(residual, residual)
        direction = residual + (norm_next / norm_now) * direction
        norm_now = norm_next
    velocity_new = velocity + TIME_STEP * solution
    spread = divergence(pad_cells(velocity_new))
    pressure = 0.4 * density * energy
    energy_lag = energy - TIME_STEP * pressure * spread / density
    moved = position + TIME_STEP * velocity_new
    free = 1.0 - pinned.astype(jnp.float32)
    relaxed = moved
    for step_index in range(SWEEPS):
        relaxed = relaxed + RELAX_RATE * free * (neighbours(pad_cells(relaxed)) / 6.0 - relaxed)
    packed = pad_cells(jnp.concatenate([relaxed - moved, density[None], (density * energy_lag)[None]]))
    remapped = remap_cells(packed)
    return velocity_new, solution, relaxed, remapped[0], remapped[1]
```

```python
import jax
import jax.numpy as jnp
from jax import lax
from jax.experimental import pallas as pl
from jax.experimental.pallas import tpu as pltpu
from jax.sharding import PartitionSpec as P

MESH = pl.DeviceIdType.MESH
F32 = jnp.float32
N = 32
LANES = 128
PX = N + 2
PY = 48
ROWS = pl.ds(8, N)
BELOW = pl.ds(7, N)
ABOVE = pl.ds(9, N)

S_P, S_RHO, S_W, S_R, S_Q, S_ONE, S_TWO, S_VEL, S_SH, S_DE = 0, 1, 2, 5, 8, 11, 14, 17, 20, 23
SLOTS = 24
E_P, E_RHO, E_VEL, E_SH = 0, 1, 2, 5
EDGES = 8


def kernel(
    sizes,
    pos_in, vel_in, rho_in, en_in, pin_in,
    v_out, a_out, r_out, d_out, e_out,
    cell, en, vel, w, r, q, nw, nr, nq, pin, free, mass, acc, one, two, de,
    ys, yr, zs, zr, exy, exz, eyz, exyz, ze, gy, mom, ar1, ar2,
    in_sem, out_sem, face_s, face_r, edge_s, edge_r, a1s, a1r, a2s, a2r,
):
    names = ("bx", "by", "bz")
    here = [lax.axis_index(name) for name in names]
    sh = q

    def exists(step):
        ok = None
        for i in range(3):
            if step[i] == 0:
                continue
            one_ok = here[i] + step[i] >= 0 if step[i] < 0 else here[i] + step[i] < sizes[i]
            ok = one_ok if ok is None else jnp.logical_and(ok, one_ok)
        return ok

    def device(step):
        return tuple(lax.rem(here[i] + step[i] + sizes[i], sizes[i]) for i in range(3))

    def flag(step):
        return exists(step).astype(jnp.int32) > 0

    def neg(step):
        return tuple(-s for s in step)

    steps = ((-1, 0, 0), (1, 0, 0), (0, -1, 0), (0, 1, 0), (0, 0, -1), (0, 0, 1))
    lane = lax.broadcasted_iota(jnp.int32, (N, LANES), 1)
    first_lane = lane == 0
    last_lane = lane == LANES - 1

    def face_copy(slot, field, d):
        if d < 2:
            src, dst = ((1, PX - 1), (N, 0))[d]
            src, dst = field.at[:, src, ROWS, :], field.at[:, dst, ROWS, :]
        elif d < 4:
            src, dst = ys.at[slot, d - 2], yr.at[slot, 3 - d]
        else:
            src, dst = zs.at[slot, d - 4], zr.at[slot, 5 - d]
        return pltpu.make_async_remote_copy(
            src_ref=src, dst_ref=dst, send_sem=face_s.at[slot, d], recv_sem=face_r.at[slot, d],
            device_id=device(steps[d]), device_id_type=MESH)

    def edge_copies(slot, eslot, sign):
        side = 1 if sign > 0 else 0
        row = N - 1 if sign > 0 else 0
        tile = pl.ds(N - 8, 8) if sign > 0 else pl.ds(0, 8)
        pieces = (
            ((sign, sign, 0), ys.at[slot, side, :, row], exy.at[eslot]),
            ((sign, 0, sign), zs.at[slot, side], exz.at[eslot]),
            ((0, sign, sign), zs.at[slot, side, tile], eyz.at[eslot]),
            ((sign, sign, sign), zs.at[slot, side, tile], exyz.at[eslot]),
        )
        return [
            (step, pltpu.make_async_remote_copy(
                src_ref=src, dst_ref=dst, send_sem=edge_s.at[eslot, i], recv_sem=edge_r.at[eslot, i],
                device_id=device(step), device_id_type=MESH))
            for i, (step, src, dst) in enumerate(pieces)
        ]

    sent = {}

    def drain(slot):
        for step, copy in sent.pop(slot):
            pl.when(exists(step))(copy.wait_send)

    def send_faces(slot, field, ds=(0, 1, 2, 3, 4, 5)):
        for d in ds:
            copy = face_copy(slot, field, d)
            pl.when(exists(steps[d]))(copy.start)
            sent.setdefault(slot, []).append((steps[d], copy))

    def send_edges(slot, eslot, sign):
        for step, copy in edge_copies(slot, eslot, sign):
            pl.when(exists(step))(copy.start)
            sent.setdefault(slot, []).append((step, copy))

    def wait_faces(slot, field, ds=(0, 1, 2, 3, 4, 5)):
        for d in ds:
            pl.when(exists(neg(steps[d])))(face_copy(slot, field, d).wait_recv)

    def wait_edges(slot, eslot, sign):
        for step, copy in edge_copies(slot, eslot, sign):
            pl.when(exists(neg(step)))(copy.wait_recv)

    def pack_rows(slot, h, x, low, high, sides=(0, 1)):
        if 0 in sides:
            ys[slot, 0, h, x] = low
        if 1 in sides:
            ys[slot, 1, h, x] = high

    def put_low(z, a, x):
        return jnp.where(lane == x + 1, pltpu.roll(a, x + 1, 1), z)

    def put_high(z, b, x):
        return jnp.where(lane == x + 1, pltpu.roll(b, x + 2, 1), z)

    zero_plane = jnp.zeros((N, LANES), F32)

    def pack(slot, field, sides=(0, 1)):
        def body(x, zz):
            low, high = zz
            for h in range(2):
                for s in sides:
                    row = 8 if s == 0 else 7 + N
                    ys[slot, s, h, x] = field[h, x + 1, row:row + 1, :]
            if 0 in sides:
                low = put_low(low, field[0, x + 1, ROWS, :], x)
            if 1 in sides:
                high = put_high(high, field[1, x + 1, ROWS, :], x)
            return low, high
        low, high = lax.fori_loop(0, N, body, (zero_plane, zero_plane), unroll=2)
        if 0 in sides:
            zs[slot, 0] = low
        if 1 in sides:
            zs[slot, 1] = high

    def unpack_rows(slot, field, sides=(0, 1)):
        have = [flag((0, -1, 0)), flag((0, 1, 0))]

        def body(x, _):
            for s in sides:
                row = 7 if s == 0 else 8 + N
                for h in range(2):
                    got = yr[slot, s, h, x]
                    field[h, x + 1, row:row + 1, :] = jnp.where(have[s], got, jnp.zeros_like(got))
            return 0
        lax.fori_loop(0, N, body, 0, unroll=4)

    def z_halo(slot, side):
        have = flag((0, 0, -1 if side == 0 else 1))
        return jnp.where(have, zr[slot, side], zero_plane)

    def edge_halo(slot, eslot, field, sign):
        side = 0 if sign > 0 else 1
        unpack_rows(slot, field, (side,))
        step = -sign
        plane, row = (0, 7) if sign > 0 else (PX - 1, 8 + N)
        have = flag((step, step, 0))
        for h in range(2):
            got = exy[eslot, h]
            field[h, plane, row:row + 1, :] = jnp.where(have, got, jnp.zeros_like(got))
        turn, at = (LANES - N, 0) if sign > 0 else (N, N + 1)
        beside = jnp.where(flag((step, 0, step)), exz[eslot], zero_plane)
        ze[eslot, ROWS, :] = jnp.where(lane == at, pltpu.roll(beside, turn, 1), z_halo(slot, side))
        tile_lane = lax.broadcasted_iota(jnp.int32, (8, LANES), 1)
        zero_tile = jnp.zeros((8, LANES), F32)
        corner = jnp.where(flag((step, step, step)), exyz[eslot], zero_tile)
        across = jnp.where(flag((0, step, step)), eyz[eslot], zero_tile)
        tile = pl.ds(0, 8) if sign > 0 else pl.ds(8 + N, 8)
        ze[eslot, tile, :] = jnp.where(tile_lane == at, pltpu.roll(corner, turn, 1), across)

    def clear_missing(field, planes=(0, PX - 1)):
        for plane in planes:
            step = (-1, 0, 0) if plane == 0 else (1, 0, 0)

            @pl.when(jnp.logical_not(exists(step)))
            def _():
                for h in range(2):
                    field[h, plane, ROWS, :] = zero_plane

    def z_below(a, b, halo):
        ra, rb = pltpu.roll(a, 1, 1), pltpu.roll(b, 1, 1)
        return jnp.where(first_lane, halo, ra), jnp.where(first_lane, ra, rb)

    def z_above(a, b, halo):
        ra, rb = pltpu.roll(a, LANES - 1, 1), pltpu.roll(b, LANES - 1, 1)
        return jnp.where(last_lane, rb, ra), jnp.where(last_lane, halo, rb)

    def to_first(z, at):
        return pltpu.roll(z, lax.rem(LANES - at, LANES), 1)

    def to_last(z, at):
        return pltpu.roll(z, LANES - 1 - at, 1)

    def neighbours(field, x, low, high):
        i = x + 1
        a, b = field[0, i, ROWS, :], field[1, i, ROWS, :]
        am, bm = z_below(a, b, to_first(low, i))
        ap, bp = z_above(a, b, to_last(high, i))
        out = []
        for h, (m, p) in enumerate(((am, ap), (bm, bp))):
            s = (field[h, i - 1, ROWS, :] + field[h, i + 1, ROWS, :]) + (
                field[h, i, BELOW, :] + field[h, i, ABOVE, :])
            out.append(s + (m + p))
        return (a, b), out

    def fold(v):
        return (v[0:8] + v[8:16]) + (v[16:24] + v[24:32])

    def halves(k):
        return pl.ds(k * LANES, LANES)

    loads = {}
    for h in range(2):
        loads["rho", h] = pltpu.make_async_copy(
            rho_in.at[:, :, halves(h)], cell.at[1, h, pl.ds(1, N), ROWS, :], in_sem.at[0, h])
        loads["en", h] = pltpu.make_async_copy(en_in.at[:, :, halves(h)], en.at[h], in_sem.at[1, h])
        loads["vel", h] = pltpu.make_async_copy(
            vel_in.at[:, :, :, halves(h)], vel.at[:, h, pl.ds(1, N), ROWS, :], in_sem.at[2, h])
        loads["pos", h] = pltpu.make_async_copy(
            pos_in.at[:, :, :, halves(h)], w.at[:, h, pl.ds(1, N), ROWS, :], in_sem.at[3, h])
        loads["pin", h] = pltpu.make_async_copy(pin_in.at[:, :, halves(h)], pin.at[h], in_sem.at[4, h])
    for name in ("rho", "en", "vel", "pos", "pin"):
        for h in range(2):
            loads[name, h].start()

    clear_missing(cell.at[0], (0,))
    clear_missing(cell.at[1])
    clear_missing(de)
    for c in range(3):
        for field in (w, r, q, one, two):
            clear_missing(field.at[c])
        clear_missing(vel.at[c], (PX - 1,))

    barrier = pltpu.get_barrier_semaphore()
    around = [s for s in ((i, j, k) for i in (0, 1) for j in (0, 1) for k in (0, 1)) if any(s)]
    around = around + [neg(s) for s in around]
    count = 0
    for step in around:
        @pl.when(exists(step))
        def _():
            pl.semaphore_signal(barrier, inc=1, device_id=device(step), device_id_type=MESH)
        count = count + exists(step).astype(jnp.int32)
    nz, nxy = sizes[2], sizes[0] * sizes[1]

    def z_peer(k):
        return (here[0], here[1], lax.rem(here[2] + k, nz))

    def xy_peer(k):
        return (lax.rem(here[0] + k // sizes[1], sizes[0]), lax.rem(here[1] + k % sizes[1], sizes[1]), here[2])

    for k in range(1, nz):
        pl.semaphore_signal(barrier, inc=1, device_id=z_peer(k), device_id_type=MESH)
    for k in range(1, nxy):
        pl.semaphore_signal(barrier, inc=1, device_id=xy_peer(k), device_id_type=MESH)

    for name in ("rho", "en"):
        for h in range(2):
            loads[name, h].wait()

    def pressure_body(x, zz):
        ph, rl, rh = zz
        for h in range(2):
            rho = cell[1, h, x + 1, ROWS, :]
            p = 0.1 * rho * en[h, x]
            cell[0, h, x + 1, ROWS, :] = p
            ys[S_P, 1, h, x] = p[N - 1:N]
            ys[S_RHO, 0, h, x] = rho[0:1]
            ys[S_RHO, 1, h, x] = rho[N - 1:N]
            if h == 0:
                rl = put_low(rl, rho, x)
            else:
                ph = put_high(ph, p, x)
                rh = put_high(rh, rho, x)
        return ph, rl, rh

    ph, rl, rh = lax.fori_loop(0, N, pressure_body, (zero_plane,) * 3)
    zs[S_P, 1] = ph
    zs[S_RHO, 0] = rl
    zs[S_RHO, 1] = rh

    pl.semaphore_wait(barrier, count + (nz - 1) + (nxy - 1))
    send_edges(S_P, E_P, 1)
    send_edges(S_RHO, E_RHO, 1)
    send_faces(S_P, cell.at[0], (5, 3, 1))
    send_faces(S_RHO, cell.at[1], (5, 3, 1, 4, 2, 0))

    for name in ("vel", "pos", "pin"):
        for h in range(2):
            loads[name, h].wait()

    def advance(c):
        def body(x, zz):
            low, high = zz
            for h in range(2):
                v = w[c, h, x + 1, ROWS, :] + 0.6 * vel[c, h, x + 1, ROWS, :]
                w[c, h, x + 1, ROWS, :] = v
                pack_rows(S_W + c, h, x, v[0:1], v[N - 1:N])
                if h == 0:
                    low = put_low(low, v, x)
                else:
                    high = put_high(high, v, x)
            return low, high
        low, high = lax.fori_loop(0, N, body, (zero_plane,) * 2)
        zs[S_W + c, 0] = low
        zs[S_W + c, 1] = high
        send_faces(S_W + c, w.at[c])

    for c in range(3):
        advance(c)

    def mask_body(x, _):
        for h in range(2):
            free[h, x] = 0.8 - 0.8 * pin[h, x].astype(F32)
        return 0
    lax.fori_loop(0, N, mask_body, 0)

    wait_faces(S_P, cell.at[0], (5, 3, 1))
    wait_edges(S_P, E_P, 1)
    wait_faces(S_RHO, cell.at[1])
    wait_edges(S_RHO, E_RHO, 1)
    edge_halo(S_P, E_P, cell.at[0], 1)
    edge_halo(S_RHO, E_RHO, cell.at[1], 1)
    unpack_rows(S_RHO, cell.at[1], (1,))
    zay = ze[E_P, ROWS, :] + ze[E_P, BELOW, :]
    zdy = ze[E_P, BELOW, :] - ze[E_P, ROWS, :]
    zrho = ze[E_RHO, ROWS, :] + ze[E_RHO, BELOW, :]

    def force_terms(i):
        ay, dy = [], []
        for h in range(2):
            c, b = cell[0, h, i, ROWS, :], cell[0, h, i, BELOW, :]
            ay.append(c + b)
            dy.append(b - c)
        aym = z_below(ay[0], ay[1], to_first(zay, i))
        dym = z_below(dy[0], dy[1], to_first(zdy, i))
        return tuple(
            t for h in range(2) for t in (ay[h] + aym[h], dy[h] + dym[h], aym[h] - ay[h]))

    def force_body(x, before):
        now = force_terms(x + 1)
        for h in range(2):
            r[0, h, x + 1, ROWS, :] = before[3 * h] - now[3 * h]
            r[1, h, x + 1, ROWS, :] = before[3 * h + 1] + now[3 * h + 1]
            r[2, h, x + 1, ROWS, :] = before[3 * h + 2] + now[3 * h + 2]
        return now
    lax.fori_loop(0, N, force_body, force_terms(0))

    for c in range(3):
        pack(S_R + c, r.at[c])
        send_faces(S_R + c, r.at[c])

    def mass_terms(i):
        ay = [cell[1, h, i, ROWS, :] + cell[1, h, i, BELOW, :] for h in range(2)]
        aym = z_below(ay[0], ay[1], to_first(zrho, i))
        return ay[0] + aym[0], ay[1] + aym[1]

    def mass_body(x, before):
        now = mass_terms(x + 1)
        for h in range(2):
            mass[h, x] = 0.125 * (before[h] + now[h]) + 1.2
        return now
    lax.fori_loop(0, N, mass_body, mass_terms(0))

    zero_tile = jnp.zeros((8, LANES), F32)

    def receive(slot, field):
        wait_faces(slot, field)
        unpack_rows(slot, field)
        return z_halo(slot, 0), z_halo(slot, 1)

    for c in range(3):
        zl, zh = receive(S_R + c, r.at[c])

        def image_body(x, carry, c=c, zl=zl, zh=zh):
            low, high, m0, m1, m2 = carry
            centre, near = neighbours(r.at[c], x, zl, zh)
            for h in range(2):
                image = mass[h, x] * centre[h] + 0.2 * near[h]
                q[c, h, x + 1, ROWS, :] = image
                nr[c, h, x] = near[h]
                m0 = m0 + fold(centre[h] * centre[h])
                m1 = m1 + fold(centre[h] * image)
                m2 = m2 + fold(image * image)
                pack_rows(S_Q + c, h, x, image[0:1], image[N - 1:N])
                if h == 0:
                    low = put_low(low, image, x)
                else:
                    high = put_high(high, image, x)
            return low, high, m0, m1, m2
        low, high, m0, m1, m2 = lax.fori_loop(
            0, N, image_body, (zero_plane, zero_plane, zero_tile, zero_tile, zero_tile))
        zs[S_Q + c, 0] = low
        zs[S_Q + c, 1] = high
        send_faces(S_Q + c, q.at[c])
        for k, m in enumerate((m0, m1, m2)):
            mom[4 * c + k:4 * c + k + 1, :] = jnp.sum(m, axis=0, keepdims=True)

    def near_w(c):
        zl, zh = receive(S_W + c, w.at[c])

        def body(x, _):
            _c, near = neighbours(w.at[c], x, zl, zh)
            for h in range(2):
                nw[c, h, x] = near[h]
            return 0
        lax.fori_loop(0, N, body, 0)

    near_w(0)
    for c in range(3):
        zl, zh = receive(S_Q + c, q.at[c])

        def second_body(x, m3, c=c, zl=zl, zh=zh):
            centre, near = neighbours(q.at[c], x, zl, zh)
            for h in range(2):
                nq[c, h, x] = near[h]
                m3 = m3 + fold(centre[h] * (mass[h, x] * centre[h] + 0.2 * near[h]))
            return m3
        m3 = lax.fori_loop(0, N, second_body, zero_tile)
        mom[4 * c + 3:4 * c + 4, :] = jnp.sum(m3, axis=0, keepdims=True)
    mom[12:16, :] = jnp.zeros((4, LANES), F32)

    total = jnp.sum(mom[...], axis=1, keepdims=True)
    on_row = lax.broadcasted_iota(jnp.int32, (16, LANES), 0)
    on_lane = lax.broadcasted_iota(jnp.int32, (16, LANES), 1)
    ar1[0] = jnp.sum(jnp.where(on_row == on_lane, total, 0.0), axis=0, keepdims=True)

    def reduce_copies(buf, send, recv, peer, peers):
        return [
            pltpu.make_async_remote_copy(
                src_ref=buf.at[0], dst_ref=buf.at[k], send_sem=send.at[k], recv_sem=recv.at[k],
                device_id=peer(k), device_id_type=MESH)
            for k in range(1, peers)
        ]

    def gathered(buf, copies):
        for copy in copies:
            copy.wait_recv()
        parts = [buf[k] for k in range(len(copies) + 1)]
        while len(parts) > 1:
            parts = [a + b for a, b in zip(parts[::2], parts[1::2])]
        return parts[0]

    along = reduce_copies(ar1, a1s, a1r, z_peer, nz)
    for copy in along:
        copy.start()
    near_w(1)
    ar2[0] = gathered(ar1, along)
    across = reduce_copies(ar2, a2s, a2r, xy_peer, nxy)
    for copy in across:
        copy.start()
    near_w(2)
    sums = gathered(ar2, across)
    row_lane = lax.broadcasted_iota(jnp.int32, (1, LANES), 1)

    def pick(k):
        return jnp.sum(jnp.where(row_lane == k, sums, 0.0), axis=1, keepdims=True)

    outs = []

    def write(src, dst, i, h):
        copy = pltpu.make_async_copy(src, dst, out_sem.at[i, h])
        copy.start()
        outs.append(copy)

    for c in range(3):
        m0, m1, m2, m3 = [pick(4 * c + k) for k in range(4)]
        a1 = m0 / m1
        new = m0 - 2.0 * a1 * m1 + a1 * a1 * m2
        b1 = 1.0 + new / m0
        a2 = new / (b1 * b1 * m1 - 2.0 * a1 * b1 * m2 + a1 * a1 * m3)
        c1 = jnp.broadcast_to(a1 + a2 * b1, (N, LANES))
        c2 = jnp.broadcast_to(-a1 * a2, (N, LANES))

        def step_body(x, carry, c=c, c1=c1, c2=c2):
            low, high = carry
            i = x + 1
            for h in range(2):
                a = c1 * r[c, h, i, ROWS, :] + c2 * q[c, h, i, ROWS, :]
                acc[c, h, x] = a
                v = vel[c, h, i, ROWS, :] + 0.6 * a
                vel[c, h, i, ROWS, :] = v
                moved = w[c, h, i, ROWS, :] + 0.36 * a
                w[c, h, i, ROWS, :] = moved
                near = nw[c, h, x] + 0.36 * (c1 * nr[c, h, x] + c2 * nq[c, h, x])
                u = moved + free[h, x] * (near * (1.0 / 6.0) - moved)
                one[c, h, i, ROWS, :] = u
                pack_rows(S_ONE + c, h, x, u[0:1], u[N - 1:N])
                if h == 0:
                    low = put_low(low, u, x)
                else:
                    high = put_high(high, u, x)
            return low, high
        drain(S_W + c)
        low, high = lax.fori_loop(0, N, step_body, (zero_plane,) * 2)
        zs[S_ONE + c, 0] = low
        zs[S_ONE + c, 1] = high
        send_faces(S_ONE + c, one.at[c])
    for c in range(3):
        pack(S_VEL + c, vel.at[c], (0,))
        send_faces(S_VEL + c, vel.at[c], (0, 2, 4))
        send_edges(S_VEL + c, E_VEL + c, -1)
        for h in range(2):
            write(acc.at[c, h], a_out.at[c, :, :, halves(h)], c, h)
            write(vel.at[c, h, pl.ds(1, N), ROWS, :], v_out.at[c, :, :, halves(h)], 3 + c, h)

    def swept(field, c, x, zl, zh):
        centre, near = neighbours(field.at[c], x, zl, zh)
        return [centre[h] + free[h, x] * (near[h] * (1.0 / 6.0) - centre[h]) for h in range(2)]

    for c in range(3):
        zl, zh = receive(S_ONE + c, one.at[c])

        def sweep_body(x, carry, c=c, zl=zl, zh=zh):
            low, high = carry
            u = swept(one, c, x, zl, zh)
            for h in range(2):
                two[c, h, x + 1, ROWS, :] = u[h]
                pack_rows(S_TWO + c, h, x, u[h][0:1], u[h][N - 1:N])
            return put_low(low, u[0], x), put_high(high, u[1], x)
        low, high = lax.fori_loop(0, N, sweep_body, (zero_plane,) * 2)
        zs[S_TWO + c, 0] = low
        zs[S_TWO + c, 1] = high
        send_faces(S_TWO + c, two.at[c])

    for c in range(3):
        wait_faces(S_VEL + c, vel.at[c], (0, 2, 4))
        wait_edges(S_VEL + c, E_VEL + c, -1)
        edge_halo(S_VEL + c, E_VEL + c, vel.at[c], -1)

    def rows_up(k):
        return ze[k, ROWS, :], ze[k, ABOVE, :]

    zx, zy, zz3 = rows_up(E_VEL), rows_up(E_VEL + 1), rows_up(E_VEL + 2)
    z_s1 = (zy[1] - zy[0]) + (zz3[0] + zz3[1])
    z_s2 = zx[0] + zx[1]

    def div_terms(i):
        s1, s2, s3 = [], [], []
        for h in range(2):
            ax = vel[0, h, i, ROWS, :] + vel[0, h, i, ABOVE, :]
            dy = vel[1, h, i, ABOVE, :] - vel[1, h, i, ROWS, :]
            az = vel[2, h, i, ROWS, :] + vel[2, h, i, ABOVE, :]
            s1.append(dy + az)
            s2.append(ax)
            s3.append(dy - az)
        u1 = z_above(s1[0], s1[1], to_last(z_s1, i))
        u2 = z_above(s2[0], s2[1], to_last(z_s2, i))
        plus, minus = [], []
        for h in range(2):
            flat, along_x = s3[h] + u1[h], s2[h] + u2[h]
            plus.append(flat + along_x)
            minus.append(flat - along_x)
        return plus, minus

    def div_body(x, carry):
        b0, b1, low, high = carry
        plus, minus = div_terms(x + 2)
        for h, before in enumerate((b0, b1)):
            spread = before + plus[h]
            value = cell[1, h, x + 1, ROWS, :] * (en[h, x] * (1.0 - 0.06 * spread))
            de[h, x + 1, ROWS, :] = value
            pack_rows(S_DE, h, x, value[0:1], value[N - 1:N])
            if h == 0:
                low = put_low(low, value, x)
            else:
                high = put_high(high, value, x)
        return minus[0], minus[1], low, high
    _plus, minus = div_terms(1)
    _0, _1, low, high = lax.fori_loop(0, N, div_body, (minus[0], minus[1], zero_plane, zero_plane))
    zs[S_DE, 0] = low
    zs[S_DE, 1] = high
    send_faces(S_DE, de)

    for c in range(3):
        zl, zh = receive(S_TWO + c, two.at[c])

        def last_body(x, low, c=c, zl=zl, zh=zh):
            u = swept(two, c, x, zl, zh)
            for h in range(2):
                nw[c, h, x] = u[h]
                s = u[h] - w[c, h, x + 1, ROWS, :]
                sh[c, h, x + 1, ROWS, :] = s
                pack_rows(S_SH + c, h, x, s[0:1], None, (0,))
                if h == 0:
                    low = put_low(low, s, x)
            return low
        drain(S_Q + c)
        zs[S_SH + c, 0] = lax.fori_loop(0, N, last_body, zero_plane)
        send_faces(S_SH + c, sh.at[c], (4, 2, 0))
        send_edges(S_SH + c, E_SH + c, -1)
        for h in range(2):
            write(nw.at[c, h], r_out.at[c, :, :, halves(h)], 6 + c, h)

    fields = (cell.at[1], de)
    slots = (S_RHO, S_DE)
    receive(S_DE, de)
    for c in range(3):
        wait_faces(S_SH + c, sh.at[c], (4, 2, 0))
        wait_edges(S_SH + c, E_SH + c, -1)
        edge_halo(S_SH + c, E_SH + c, sh.at[c], -1)
    zx, zz3 = rows_up(E_SH), rows_up(E_SH + 2)
    z_ax = zx[0] + zx[1]
    wide = pl.ds(8, 40)
    z_y = ze[E_SH + 1, wide, :]
    z_y = z_y + pltpu.roll(z_y, LANES - 1, 1)
    z_z = zz3[0] + zz3[1]
    z_z = 0.25 * (z_z + pltpu.roll(z_z, LANES - 1, 1))
    low_q = [z_halo(slot, 0) for slot in slots]
    top_g = [z_z * jnp.where(z_z > 0, z_halo(slot, 1), zs[slot, 1]) for slot in slots]
    wide_last = lax.broadcasted_iota(jnp.int32, (40, LANES), 1) == LANES - 1

    def flux_x(i):
        a = [sh[0, h, i, ROWS, :] + sh[0, h, i, ABOVE, :] for h in range(2)]
        up = z_above(a[0], a[1], to_last(z_ax, i))
        out = []
        for h in range(2):
            s = 0.25 * (a[h] + up[h])
            for field in fields:
                out.append(s * jnp.where(s > 0, field[h, i, ROWS, :], field[h, i - 1, ROWS, :]))
        return tuple(out)

    def remap_body(x, before):
        i = x + 1
        now = flux_x(i + 1)
        t = [sh[1, h, i, wide, :] + sh[1, h, i + 1, wide, :] for h in range(2)]
        ra, rb = [pltpu.roll(v, LANES - 1, 1) for v in t]
        up = (jnp.where(wide_last, rb, ra), jnp.where(wide_last, to_last(z_y, i), rb))
        for h in range(2):
            s = 0.25 * (t[h] + up[h])
            for f, field in enumerate(fields):
                gy[f, h] = s * jnp.where(s > 0, field[h, i, wide, :], field[h, i, pl.ds(7, 40), :])
        s = [
            0.25 * ((sh[2, h, i, ROWS, :] + sh[2, h, i, ABOVE, :])
                    + (sh[2, h, i + 1, ROWS, :] + sh[2, h, i + 1, ABOVE, :]))
            for h in range(2)
        ]
        for f, field in enumerate(fields):
            own = [field[h, i, ROWS, :] for h in range(2)]
            under = z_below(own[0], own[1], to_first(low_q[f], i))
            g = [s[h] * jnp.where(s[h] > 0, own[h], under[h]) for h in range(2)]
            over = z_above(g[0], g[1], to_last(top_g[f], i))
            for h in range(2):
                nr[f, h, x] = (
                    own[h] + (now[2 * h + f] - before[2 * h + f])
                    + (gy[f, h, 1:N + 1, :] - gy[f, h, 0:N, :]) + (over[h] - g[h]))
        return now
    lax.fori_loop(0, N, remap_body, flux_x(1))
    for f, out in enumerate((d_out, e_out)):
        for h in range(2):
            write(nr.at[f, h], out.at[:, :, halves(h)], 9 + f, h)

    for slot in tuple(sent):
        drain(slot)
    for copy in along + across:
        copy.wait_send()
    for copy in outs:
        copy.wait()


def solution(mesh):
    sizes = tuple(mesh.shape[name] for name in ("bx", "by", "bz"))
    vector = P(None, "bx", "by", "bz")
    scalar = P("bx", "by", "bz")

    def on_device(position, velocity, density, energy, pinned):
        def padded(*lead):
            return pltpu.VMEM(lead + (2, PX, PY, LANES), F32)

        def plain(*lead, dtype=F32):
            return pltpu.VMEM(lead + (2, N, N, LANES), dtype)

        dma = pltpu.SemaphoreType.DMA
        v3 = jax.ShapeDtypeStruct(position.shape, F32)
        v1 = jax.ShapeDtypeStruct(density.shape, F32)
        anywhere = pl.BlockSpec(memory_space=pl.ANY)

        def body(*refs):
            kernel(sizes, *refs)

        return tuple(pl.pallas_call(
            body,
            name="lagrangian_step",
            out_shape=(v3, v3, v3, v1, v1),
            in_specs=[anywhere] * 5,
            out_specs=[anywhere] * 5,
            scratch_shapes=[
                padded(2), plain(), padded(3), padded(3), padded(3), padded(3),
                plain(3), plain(3), plain(3), plain(dtype=jnp.int32), plain(), plain(), plain(3),
                padded(3), padded(3), padded(),
                pltpu.VMEM((SLOTS, 2, 2, N, 1, LANES), F32),
                pltpu.VMEM((SLOTS, 2, 2, N, 1, LANES), F32),
                pltpu.VMEM((SLOTS, 2, N, LANES), F32),
                pltpu.VMEM((SLOTS, 2, N, LANES), F32),
                pltpu.VMEM((EDGES, 2, 1, LANES), F32),
                pltpu.VMEM((EDGES, N, LANES), F32),
                pltpu.VMEM((EDGES, 8, LANES), F32),
                pltpu.VMEM((EDGES, 8, LANES), F32),
                pltpu.VMEM((EDGES, PY, LANES), F32),
                pltpu.VMEM((2, 2, 40, LANES), F32),
                pltpu.VMEM((16, LANES), F32),
                pltpu.VMEM((sizes[2], 1, LANES), F32),
                pltpu.VMEM((sizes[0] * sizes[1], 1, LANES), F32),
                dma((5, 2)), dma((11, 2)),
                dma((SLOTS, 6)), dma((SLOTS, 6)), dma((EDGES, 4)), dma((EDGES, 4)),
                dma((sizes[2],)), dma((sizes[2],)),
                dma((sizes[0] * sizes[1],)), dma((sizes[0] * sizes[1],)),
            ],
            compiler_params=pltpu.CompilerParams(
                collective_id=0, has_side_effects=True, vmem_limit_bytes=66 * 1000 * 1000),
        )(position, velocity, density, energy, pinned))

    return jax.shard_map(
        on_device,
        mesh=mesh,
        in_specs=(vector, vector, scalar, scalar, scalar),
        out_specs=(vector, vector, vector, scalar, scalar),
        check_vma=False,
    )
```

```python
import jax
import jax.numpy as jnp
from jax import lax
from jax.experimental import pallas as pl
from jax.experimental.pallas import tpu as pltpu
from jax.sharding import PartitionSpec as P

MESH = pl.DeviceIdType.MESH
F32 = jnp.float32
N = 32
LANES = 128
PX = N + 2
PY = 48
ROWS = pl.ds(8, N)
BELOW = pl.ds(7, N)
ABOVE = pl.ds(9, N)

S_P, S_RHO, S_W, S_R, S_Q, S_ONE, S_TWO, S_VEL, S_SH, S_DE = 0, 1, 2, 5, 8, 11, 14, 17, 20, 23
SLOTS = 24
E_P, E_RHO, E_VEL, E_SH = 0, 1, 2, 5
EDGES = 8


def kernel(
    sizes,
    pos_in, vel_in, rho_in, en_in, pin_in,
    v_out, a_out, r_out, d_out, e_out,
    cell, en, vel, w, r, q, nw, nr, nq, pin, free, mass, acc, one, two, de,
    ys, yr, zs, zr, exy, exz, eyz, exyz, ze, gy, mom, ar1, ar2,
    in_sem, out_sem, face_s, face_r, edge_s, edge_r, a1s, a1r, a2s, a2r,
):
    names = ("bx", "by", "bz")
    here = [lax.axis_index(name) for name in names]
    sh = q

    def exists(step):
        ok = None
        for i in range(3):
            if step[i] == 0:
                continue
            one_ok = here[i] + step[i] >= 0 if step[i] < 0 else here[i] + step[i] < sizes[i]
            ok = one_ok if ok is None else jnp.logical_and(ok, one_ok)
        return ok

    def device(step):
        return tuple(lax.rem(here[i] + step[i] + sizes[i], sizes[i]) for i in range(3))

    def flag(step):
        return exists(step).astype(jnp.int32) > 0

    def neg(step):
        return tuple(-s for s in step)

    steps = ((-1, 0, 0), (1, 0, 0), (0, -1, 0), (0, 1, 0), (0, 0, -1), (0, 0, 1))
    lane = lax.broadcasted_iota(jnp.int32, (N, LANES), 1)
    first_lane = lane == 0
    last_lane = lane == LANES - 1

    def face_copy(slot, field, d):
        if d < 2:
            src, dst = ((1, PX - 1), (N, 0))[d]
            src, dst = field.at[:, src, ROWS, :], field.at[:, dst, ROWS, :]
        elif d < 4:
            src, dst = ys.at[slot, d - 2], yr.at[slot, 3 - d]
        else:
            src, dst = zs.at[slot], zr.at[slot, 5 - d]
        return pltpu.make_async_remote_copy(
            src_ref=src, dst_ref=dst, send_sem=face_s.at[slot, d], recv_sem=face_r.at[slot, d],
            device_id=device(steps[d]), device_id_type=MESH)

    def edge_copies(slot, eslot, sign):
        side = 1 if sign > 0 else 0
        row = N - 1 if sign > 0 else 0
        tile = pl.ds(N - 8, 8) if sign > 0 else pl.ds(0, 8)
        pieces = (
            ((sign, sign, 0), ys.at[slot, side, :, row], exy.at[eslot]),
            ((sign, 0, sign), zs.at[slot], exz.at[eslot]),
            ((0, sign, sign), zs.at[slot, tile], eyz.at[eslot]),
            ((sign, sign, sign), zs.at[slot, tile], exyz.at[eslot]),
        )
        return [
            (step, pltpu.make_async_remote_copy(
                src_ref=src, dst_ref=dst, send_sem=edge_s.at[eslot, i], recv_sem=edge_r.at[eslot, i],
                device_id=device(step), device_id_type=MESH))
            for i, (step, src, dst) in enumerate(pieces)
        ]

    sent = {}

    def drain(slot):
        for step, copy in sent.pop(slot):
            pl.when(exists(step))(copy.wait_send)

    def send_faces(slot, field, ds=(0, 1, 2, 3, 4, 5)):
        for d in ds:
            copy = face_copy(slot, field, d)
            pl.when(exists(steps[d]))(copy.start)
            sent.setdefault(slot, []).append((steps[d], copy))

    def send_edges(slot, eslot, sign):
        for step, copy in edge_copies(slot, eslot, sign):
            pl.when(exists(step))(copy.start)
            sent.setdefault(slot, []).append((step, copy))

    def wait_faces(slot, field, ds=(0, 1, 2, 3, 4, 5)):
        for d in ds:
            pl.when(exists(neg(steps[d])))(face_copy(slot, field, d).wait_recv)

    def wait_edges(slot, eslot, sign):
        for step, copy in edge_copies(slot, eslot, sign):
            pl.when(exists(neg(step)))(copy.wait_recv)

    zero_plane = jnp.zeros((N, LANES), F32)
    odd = lane % 2 == 1
    left = lane < LANES // 2

    def planes(body, init=0, trip=4):
        def run(i, carry):
            return body([i * trip + j for j in range(trip)], carry)
        return lax.fori_loop(0, N // trip, run, init)

    def lagging(xs):
        back = jnp.minimum(xs[0], len(xs))
        return [x - back for x in xs]

    def pack_planes(slot, field, xs):
        mixed = [
            pltpu.roll(jnp.where(left, field[0, x + 1, ROWS, :], field[1, x + 1, ROWS, :]), 2 * x + 3, 1)
            for x in xs
        ]
        z = zs[slot]
        for x, m in zip(xs, mixed):
            z = jnp.where((lane >> 1) == x + 1, m, z)
        zs[slot] = z

    def pack_last(slot, field, trip=4):
        pack_planes(slot, field, list(range(N - trip, N)))

    def pack_rows(slot, h, x, v, sides=(0, 1)):
        if 0 in sides:
            ys[slot, 0, h, x] = v[0:1]
        if 1 in sides:
            ys[slot, 1, h, x] = v[N - 1:N]

    def pack(slot, field, sides=(0, 1)):
        def body(xs, carry):
            pack_planes(slot, field, xs)
            for x in xs:
                for h in range(2):
                    for s in sides:
                        row = 8 if s == 0 else 7 + N
                        ys[slot, s, h, x] = field[h, x + 1, row:row + 1, :]
            return carry
        planes(body, 0, 8)

    def unpack_rows(slot, field, sides=(0, 1)):
        have = [flag((0, -1, 0)), flag((0, 1, 0))]

        def body(x, _):
            for s in sides:
                row = 7 if s == 0 else 8 + N
                for h in range(2):
                    got = yr[slot, s, h, x]
                    field[h, x + 1, row:row + 1, :] = jnp.where(have[s], got, jnp.zeros_like(got))
            return 0
        lax.fori_loop(0, N, body, 0, unroll=4)

    def z_halo(slot, side):
        have = flag((0, 0, -1 if side == 0 else 1))
        return jnp.where(have, pltpu.roll(zr[slot, side], 1 if side == 0 else LANES - 1, 1), zero_plane)

    def z_halos(slot):
        return jnp.where(odd, z_halo(slot, 0), z_halo(slot, 1))

    def edge_halo(slot, eslot, field, sign):
        side = 0 if sign > 0 else 1
        unpack_rows(slot, field, (side,))
        step = -sign
        plane, row = (0, 7) if sign > 0 else (PX - 1, 8 + N)
        have = flag((step, step, 0))
        for h in range(2):
            got = exy[eslot, h]
            field[h, plane, row:row + 1, :] = jnp.where(have, got, jnp.zeros_like(got))
        turn, at = (LANES // 2 + 1, 1) if sign > 0 else (2 * N - 1, 2 * N + 2)
        whole = 1 if sign > 0 else LANES - 1
        beside = jnp.where(flag((step, 0, step)), exz[eslot], zero_plane)
        ze[eslot, ROWS, :] = jnp.where(lane == at, pltpu.roll(beside, turn, 1), z_halo(slot, side))
        tile_lane = lax.broadcasted_iota(jnp.int32, (8, LANES), 1)
        zero_tile = jnp.zeros((8, LANES), F32)
        corner = jnp.where(flag((step, step, step)), exyz[eslot], zero_tile)
        across = jnp.where(flag((0, step, step)), eyz[eslot], zero_tile)
        tile = pl.ds(0, 8) if sign > 0 else pl.ds(8 + N, 8)
        ze[eslot, tile, :] = jnp.where(
            tile_lane == at, pltpu.roll(corner, turn, 1), pltpu.roll(across, whole, 1))

    def clear_missing(field, planes=(0, PX - 1)):
        for plane in planes:
            step = (-1, 0, 0) if plane == 0 else (1, 0, 0)

            @pl.when(jnp.logical_not(exists(step)))
            def _():
                for h in range(2):
                    field[h, plane, ROWS, :] = zero_plane

    def z_below(a, b, halo):
        ra, rb = pltpu.roll(a, 1, 1), pltpu.roll(b, 1, 1)
        return jnp.where(first_lane, halo, ra), jnp.where(first_lane, ra, rb)

    def z_above(a, b, halo):
        ra, rb = pltpu.roll(a, LANES - 1, 1), pltpu.roll(b, LANES - 1, 1)
        return jnp.where(last_lane, rb, ra), jnp.where(last_lane, halo, rb)

    def to_ends(z, i):
        return pltpu.roll(z, LANES - 1 - 2 * i, 1)

    def to_last(z, i):
        return pltpu.roll(z, LANES - 1 - 2 * i, 1)

    def to_first(z, i):
        return pltpu.roll(z, LANES - 1 - 2 * i, 1)

    def neighbours(field, xs, ends):
        rolled = []
        for x in xs:
            a, b = field[0, x + 1, ROWS, :], field[1, x + 1, ROWS, :]
            end = to_ends(ends, x + 1)
            rolled.append((z_below(a, b, end), z_above(a, b, end)))
        out = []
        for x, (m, p) in zip(xs, rolled):
            i = x + 1
            centre = [field[h, i, ROWS, :] for h in range(2)]
            near = []
            for h in range(2):
                s = (field[h, i - 1, ROWS, :] + field[h, i + 1, ROWS, :]) + (
                    field[h, i, BELOW, :] + field[h, i, ABOVE, :])
                near.append(s + (m[h] + p[h]))
            out.append((x, centre, near))
        return out

    def fold(v):
        return (v[0:8] + v[8:16]) + (v[16:24] + v[24:32])

    def halves(k):
        return pl.ds(k * LANES, LANES)

    loads = {}
    for h in range(2):
        loads["rho", h] = pltpu.make_async_copy(
            rho_in.at[:, :, halves(h)], cell.at[1, h, pl.ds(1, N), ROWS, :], in_sem.at[0, h])
        loads["en", h] = pltpu.make_async_copy(en_in.at[:, :, halves(h)], en.at[h], in_sem.at[1, h])
        loads["vel", h] = pltpu.make_async_copy(
            vel_in.at[:, :, :, halves(h)], vel.at[:, h, pl.ds(1, N), ROWS, :], in_sem.at[2, h])
        loads["pos", h] = pltpu.make_async_copy(
            pos_in.at[:, :, :, halves(h)], w.at[:, h, pl.ds(1, N), ROWS, :], in_sem.at[3, h])
        loads["pin", h] = pltpu.make_async_copy(pin_in.at[:, :, halves(h)], pin.at[h], in_sem.at[4, h])
    for name in ("rho", "en", "vel", "pos", "pin"):
        for h in range(2):
            loads[name, h].start()

    clear_missing(cell.at[0], (0,))
    clear_missing(cell.at[1])
    clear_missing(de)
    for c in range(3):
        for field in (w, r, q, one, two):
            clear_missing(field.at[c])
        clear_missing(vel.at[c], (PX - 1,))

    barrier = pltpu.get_barrier_semaphore()
    around = [s for s in ((i, j, k) for i in (0, 1) for j in (0, 1) for k in (0, 1)) if any(s)]
    around = around + [neg(s) for s in around]
    count = 0
    for step in around:
        @pl.when(exists(step))
        def _():
            pl.semaphore_signal(barrier, inc=1, device_id=device(step), device_id_type=MESH)
        count = count + exists(step).astype(jnp.int32)
    nz, nxy = sizes[2], sizes[0] * sizes[1]

    def z_peer(k):
        return (here[0], here[1], lax.rem(here[2] + k, nz))

    def xy_peer(k):
        return (lax.rem(here[0] + k // sizes[1], sizes[0]), lax.rem(here[1] + k % sizes[1], sizes[1]), here[2])

    for k in range(1, nz):
        pl.semaphore_signal(barrier, inc=1, device_id=z_peer(k), device_id_type=MESH)
    for k in range(1, nxy):
        pl.semaphore_signal(barrier, inc=1, device_id=xy_peer(k), device_id_type=MESH)

    for name in ("rho", "en"):
        for h in range(2):
            loads[name, h].wait()

    def pressure_body(xs, carry):
        back = lagging(xs)
        pack_planes(S_P, cell.at[0], back)
        pack_planes(S_RHO, cell.at[1], xs)
        for x in xs:
            for h in range(2):
                rho = cell[1, h, x + 1, ROWS, :]
                p = 0.1 * rho * en[h, x]
                cell[0, h, x + 1, ROWS, :] = p
                pack_rows(S_P, h, x, p, (1,))
                pack_rows(S_RHO, h, x, rho)
        return carry

    planes(pressure_body)
    pack_last(S_P, cell.at[0])

    pl.semaphore_wait(barrier, count + (nz - 1) + (nxy - 1))
    send_edges(S_P, E_P, 1)
    send_edges(S_RHO, E_RHO, 1)
    send_faces(S_P, cell.at[0], (5, 3, 1))
    send_faces(S_RHO, cell.at[1], (5, 3, 1, 4, 2, 0))

    for name in ("vel", "pos", "pin"):
        for h in range(2):
            loads[name, h].wait()

    def advance(c):
        def body(xs, carry):
            pack_planes(S_W + c, w.at[c], lagging(xs))
            for x in xs:
                for h in range(2):
                    v = w[c, h, x + 1, ROWS, :] + 0.6 * vel[c, h, x + 1, ROWS, :]
                    w[c, h, x + 1, ROWS, :] = v
                    pack_rows(S_W + c, h, x, v)
            return carry
        planes(body)
        pack_last(S_W + c, w.at[c])
        send_faces(S_W + c, w.at[c])

    for c in range(3):
        advance(c)

    def mask_body(x, _):
        for h in range(2):
            free[h, x] = 0.8 - 0.8 * pin[h, x].astype(F32)
        return 0
    lax.fori_loop(0, N, mask_body, 0)

    wait_faces(S_P, cell.at[0], (5, 3, 1))
    wait_edges(S_P, E_P, 1)
    wait_faces(S_RHO, cell.at[1])
    wait_edges(S_RHO, E_RHO, 1)
    edge_halo(S_P, E_P, cell.at[0], 1)
    edge_halo(S_RHO, E_RHO, cell.at[1], 1)
    unpack_rows(S_RHO, cell.at[1], (1,))
    zay = ze[E_P, ROWS, :] + ze[E_P, BELOW, :]
    zdy = ze[E_P, BELOW, :] - ze[E_P, ROWS, :]
    zrho = ze[E_RHO, ROWS, :] + ze[E_RHO, BELOW, :]

    def force_terms(i):
        ay, dy = [], []
        for h in range(2):
            c, b = cell[0, h, i, ROWS, :], cell[0, h, i, BELOW, :]
            ay.append(c + b)
            dy.append(b - c)
        aym = z_below(ay[0], ay[1], to_first(zay, i))
        dym = z_below(dy[0], dy[1], to_first(zdy, i))
        return tuple(
            t for h in range(2) for t in (ay[h] + aym[h], dy[h] + dym[h], aym[h] - ay[h]))

    def force_body(i, before):
        terms = [before] + [force_terms(4 * i + j + 1) for j in range(4)]
        for j in range(4):
            old, now = terms[j], terms[j + 1]
            for h in range(2):
                r[0, h, 4 * i + j + 1, ROWS, :] = old[3 * h] - now[3 * h]
                r[1, h, 4 * i + j + 1, ROWS, :] = old[3 * h + 1] + now[3 * h + 1]
                r[2, h, 4 * i + j + 1, ROWS, :] = old[3 * h + 2] + now[3 * h + 2]
        return terms[4]
    lax.fori_loop(0, N // 4, force_body, force_terms(0))

    for c in range(3):
        pack(S_R + c, r.at[c])
        send_faces(S_R + c, r.at[c])

    def mass_terms(i):
        ay = [cell[1, h, i, ROWS, :] + cell[1, h, i, BELOW, :] for h in range(2)]
        aym = z_below(ay[0], ay[1], to_first(zrho, i))
        return ay[0] + aym[0], ay[1] + aym[1]

    def mass_body(i, before):
        terms = [before] + [mass_terms(4 * i + j + 1) for j in range(4)]
        for j in range(4):
            for h in range(2):
                mass[h, 4 * i + j] = 0.125 * (terms[j][h] + terms[j + 1][h]) + 1.2
        return terms[4]
    lax.fori_loop(0, N // 4, mass_body, mass_terms(0))

    zero_tile = jnp.zeros((8, LANES), F32)

    def receive(slot, field):
        wait_faces(slot, field)
        unpack_rows(slot, field)
        return z_halos(slot)

    for c in range(3):
        ends = receive(S_R + c, r.at[c])

        def image_body(xs, carry, c=c, ends=ends):
            m0, m1, m2 = carry
            pack_planes(S_Q + c, q.at[c], lagging(xs))
            for x, centre, near in neighbours(r.at[c], xs, ends):
                for h in range(2):
                    image = mass[h, x] * centre[h] + 0.2 * near[h]
                    q[c, h, x + 1, ROWS, :] = image
                    nr[c, h, x] = near[h]
                    m0 = m0 + fold(centre[h] * centre[h])
                    m1 = m1 + fold(centre[h] * image)
                    m2 = m2 + fold(image * image)
                    pack_rows(S_Q + c, h, x, image)
            return m0, m1, m2
        moments = planes(image_body, (zero_tile, zero_tile, zero_tile))
        pack_last(S_Q + c, q.at[c])
        send_faces(S_Q + c, q.at[c])
        for k, m in enumerate(moments):
            mom[4 * c + k:4 * c + k + 1, :] = jnp.sum(m, axis=0, keepdims=True)

    def near_w(c):
        ends = receive(S_W + c, w.at[c])

        def body(xs, carry):
            for x, _centre, near in neighbours(w.at[c], xs, ends):
                for h in range(2):
                    nw[c, h, x] = near[h]
            return carry
        planes(body)

    near_w(0)
    for c in range(3):
        ends = receive(S_Q + c, q.at[c])

        def second_body(xs, m3, c=c, ends=ends):
            for x, centre, near in neighbours(q.at[c], xs, ends):
                for h in range(2):
                    nq[c, h, x] = near[h]
                    m3 = m3 + fold(centre[h] * (mass[h, x] * centre[h] + 0.2 * near[h]))
            return m3
        m3 = planes(second_body, zero_tile)
        mom[4 * c + 3:4 * c + 4, :] = jnp.sum(m3, axis=0, keepdims=True)
    mom[12:16, :] = jnp.zeros((4, LANES), F32)

    total = jnp.sum(mom[...], axis=1, keepdims=True)
    on_row = lax.broadcasted_iota(jnp.int32, (16, LANES), 0)
    on_lane = lax.broadcasted_iota(jnp.int32, (16, LANES), 1)
    ar1[0] = jnp.sum(jnp.where(on_row == on_lane, total, 0.0), axis=0, keepdims=True)

    def reduce_copies(buf, send, recv, peer, peers):
        return [
            pltpu.make_async_remote_copy(
                src_ref=buf.at[0], dst_ref=buf.at[k], send_sem=send.at[k], recv_sem=recv.at[k],
                device_id=peer(k), device_id_type=MESH)
            for k in range(1, peers)
        ]

    def gathered(buf, copies):
        for copy in copies:
            copy.wait_recv()
        parts = [buf[k] for k in range(len(copies) + 1)]
        while len(parts) > 1:
            parts = [a + b for a, b in zip(parts[::2], parts[1::2])]
        return parts[0]

    along = reduce_copies(ar1, a1s, a1r, z_peer, nz)
    for copy in along:
        copy.start()
    near_w(1)
    ar2[0] = gathered(ar1, along)
    across = reduce_copies(ar2, a2s, a2r, xy_peer, nxy)
    for copy in across:
        copy.start()
    near_w(2)
    sums = gathered(ar2, across)
    row_lane = lax.broadcasted_iota(jnp.int32, (1, LANES), 1)

    def pick(k):
        return jnp.sum(jnp.where(row_lane == k, sums, 0.0), axis=1, keepdims=True)

    outs = []

    def write(src, dst, i, h):
        copy = pltpu.make_async_copy(src, dst, out_sem.at[i, h])
        copy.start()
        outs.append(copy)

    for c in range(3):
        m0, m1, m2, m3 = [pick(4 * c + k) for k in range(4)]
        a1 = m0 / m1
        new = m0 - 2.0 * a1 * m1 + a1 * a1 * m2
        b1 = 1.0 + new / m0
        a2 = new / (b1 * b1 * m1 - 2.0 * a1 * b1 * m2 + a1 * a1 * m3)
        c1 = jnp.broadcast_to(a1 + a2 * b1, (N, LANES))
        c2 = jnp.broadcast_to(-a1 * a2, (N, LANES))

        def step_body(xs, carry, c=c, c1=c1, c2=c2):
            pack_planes(S_ONE + c, one.at[c], lagging(xs))
            for x in xs:
                i = x + 1
                for h in range(2):
                    a = c1 * r[c, h, i, ROWS, :] + c2 * q[c, h, i, ROWS, :]
                    acc[c, h, x] = a
                    v = vel[c, h, i, ROWS, :] + 0.6 * a
                    vel[c, h, i, ROWS, :] = v
                    moved = w[c, h, i, ROWS, :] + 0.36 * a
                    w[c, h, i, ROWS, :] = moved
                    near = nw[c, h, x] + 0.36 * (c1 * nr[c, h, x] + c2 * nq[c, h, x])
                    u = moved + free[h, x] * (near * (1.0 / 6.0) - moved)
                    one[c, h, i, ROWS, :] = u
                    pack_rows(S_ONE + c, h, x, u)
            return carry
        drain(S_W + c)
        planes(step_body)
        pack_last(S_ONE + c, one.at[c])
        send_faces(S_ONE + c, one.at[c])
    for c in range(3):
        pack(S_VEL + c, vel.at[c], (0,))
        send_faces(S_VEL + c, vel.at[c], (0, 2, 4))
        send_edges(S_VEL + c, E_VEL + c, -1)
        for h in range(2):
            write(acc.at[c, h], a_out.at[c, :, :, halves(h)], c, h)
            write(vel.at[c, h, pl.ds(1, N), ROWS, :], v_out.at[c, :, :, halves(h)], 3 + c, h)

    def swept(field, c, xs, ends):
        return [
            (x, [centre[h] + free[h, x] * (near[h] * (1.0 / 6.0) - centre[h]) for h in range(2)])
            for x, centre, near in neighbours(field.at[c], xs, ends)
        ]

    for c in range(3):
        ends = receive(S_ONE + c, one.at[c])

        def sweep_body(xs, carry, c=c, ends=ends):
            pack_planes(S_TWO + c, two.at[c], lagging(xs))
            for x, u in swept(one, c, xs, ends):
                for h in range(2):
                    two[c, h, x + 1, ROWS, :] = u[h]
                    pack_rows(S_TWO + c, h, x, u[h])
            return carry
        planes(sweep_body)
        pack_last(S_TWO + c, two.at[c])
        send_faces(S_TWO + c, two.at[c])

    for c in range(3):
        wait_faces(S_VEL + c, vel.at[c], (0, 2, 4))
        wait_edges(S_VEL + c, E_VEL + c, -1)
        edge_halo(S_VEL + c, E_VEL + c, vel.at[c], -1)

    def rows_up(k):
        return ze[k, ROWS, :], ze[k, ABOVE, :]

    zx, zy, zz3 = rows_up(E_VEL), rows_up(E_VEL + 1), rows_up(E_VEL + 2)
    z_s1 = (zy[1] - zy[0]) + (zz3[0] + zz3[1])
    z_s2 = zx[0] + zx[1]

    def div_terms(i):
        s1, s2, s3 = [], [], []
        for h in range(2):
            ax = vel[0, h, i, ROWS, :] + vel[0, h, i, ABOVE, :]
            dy = vel[1, h, i, ABOVE, :] - vel[1, h, i, ROWS, :]
            az = vel[2, h, i, ROWS, :] + vel[2, h, i, ABOVE, :]
            s1.append(dy + az)
            s2.append(ax)
            s3.append(dy - az)
        u1 = z_above(s1[0], s1[1], to_last(z_s1, i))
        u2 = z_above(s2[0], s2[1], to_last(z_s2, i))
        plus, minus = [], []
        for h in range(2):
            flat, along_x = s3[h] + u1[h], s2[h] + u2[h]
            plus.append(flat + along_x)
            minus.append(flat - along_x)
        return plus, minus

    def div_body(k, before):
        back = jnp.maximum(2 * k - 2, 0)
        pack_planes(S_DE, de, [back, back + 1])
        for j in range(2):
            x = 2 * k + j
            plus, minus = div_terms(x + 2)
            for h in range(2):
                spread = before[h] + plus[h]
                value = cell[1, h, x + 1, ROWS, :] * (en[h, x] * (1.0 - 0.06 * spread))
                de[h, x + 1, ROWS, :] = value
                pack_rows(S_DE, h, x, value)
            before = minus
        return tuple(before)
    lax.fori_loop(0, N // 2, div_body, tuple(div_terms(1)[1]))
    pack_last(S_DE, de, 2)
    send_faces(S_DE, de)

    for c in range(3):
        ends = receive(S_TWO + c, two.at[c])
        drain(S_Q + c)

        def last_body(xs, carry, c=c, ends=ends):
            pack_planes(S_SH + c, sh.at[c], lagging(xs))
            for x, u in swept(two, c, xs, ends):
                for h in range(2):
                    nw[c, h, x] = u[h]
                    s = u[h] - w[c, h, x + 1, ROWS, :]
                    sh[c, h, x + 1, ROWS, :] = s
                    pack_rows(S_SH + c, h, x, s, (0,))
            return carry
        planes(last_body)
        pack_last(S_SH + c, sh.at[c])
        send_faces(S_SH + c, sh.at[c], (4, 2, 0))
        send_edges(S_SH + c, E_SH + c, -1)
        for h in range(2):
            write(nw.at[c, h], r_out.at[c, :, :, halves(h)], 6 + c, h)

    fields = (cell.at[1], de)
    slots = (S_RHO, S_DE)
    receive(S_DE, de)
    for c in range(3):
        wait_faces(S_SH + c, sh.at[c], (4, 2, 0))
        wait_edges(S_SH + c, E_SH + c, -1)
        edge_halo(S_SH + c, E_SH + c, sh.at[c], -1)
    zx, zz3 = rows_up(E_SH), rows_up(E_SH + 2)
    z_ax = zx[0] + zx[1]
    wide = pl.ds(8, 40)
    z_y = ze[E_SH + 1, wide, :]
    z_y = z_y + pltpu.roll(z_y, LANES - 2, 1)
    z_z = zz3[0] + zz3[1]
    z_z = 0.25 * (z_z + pltpu.roll(z_z, LANES - 2, 1))
    ends_q = [
        jnp.where(odd, z_halo(slot, 0), z_z * jnp.where(z_z > 0, z_halo(slot, 1), zs[slot]))
        for slot in slots
    ]
    wide_last = lax.broadcasted_iota(jnp.int32, (40, LANES), 1) == LANES - 1

    def flux_x(i):
        a = [sh[0, h, i, ROWS, :] + sh[0, h, i, ABOVE, :] for h in range(2)]
        up = z_above(a[0], a[1], to_last(z_ax, i))
        out = []
        for h in range(2):
            s = 0.25 * (a[h] + up[h])
            for field in fields:
                out.append(s * jnp.where(s > 0, field[h, i, ROWS, :], field[h, i - 1, ROWS, :]))
        return tuple(out)

    def remap_x(k, before):
        for j in range(2):
            x = 2 * k + j
            now = flux_x(x + 2)
            for h in range(2):
                for f, field in enumerate(fields):
                    nr[f, h, x] = field[h, x + 1, ROWS, :] + (now[2 * h + f] - before[2 * h + f])
            before = now
        return before
    lax.fori_loop(0, N // 2, remap_x, flux_x(1))

    def remap_y(xs, carry):
        for j, x in enumerate(xs):
            i = x + 1
            t = [sh[1, h, i, wide, :] + sh[1, h, i + 1, wide, :] for h in range(2)]
            ra, rb = [pltpu.roll(v, LANES - 1, 1) for v in t]
            up = (jnp.where(wide_last, rb, ra), jnp.where(wide_last, to_last(z_y, i), rb))
            for h in range(2):
                s = 0.25 * (t[h] + up[h])
                for f, field in enumerate(fields):
                    gy[j, f, h] = s * jnp.where(s > 0, field[h, i, wide, :], field[h, i, pl.ds(7, 40), :])
        for j, x in enumerate(xs):
            for h in range(2):
                for f in range(2):
                    nr[f, h, x] = nr[f, h, x] + (gy[j, f, h, 1:N + 1, :] - gy[j, f, h, 0:N, :])
        return carry
    planes(remap_y, 0, 2)

    def remap_z(xs, carry):
        for x in xs:
            i = x + 1
            s = [
                0.25 * ((sh[2, h, i, ROWS, :] + sh[2, h, i, ABOVE, :])
                        + (sh[2, h, i + 1, ROWS, :] + sh[2, h, i + 1, ABOVE, :]))
                for h in range(2)
            ]
            for f, field in enumerate(fields):
                own = [field[h, i, ROWS, :] for h in range(2)]
                end = to_ends(ends_q[f], i)
                under = z_below(own[0], own[1], end)
                g = [s[h] * jnp.where(s[h] > 0, own[h], under[h]) for h in range(2)]
                over = z_above(g[0], g[1], end)
                for h in range(2):
                    nr[f, h, x] = nr[f, h, x] + (over[h] - g[h])
        return carry
    planes(remap_z, 0, 2)
    for f, out in enumerate((d_out, e_out)):
        for h in range(2):
            write(nr.at[f, h], out.at[:, :, halves(h)], 9 + f, h)

    for slot in tuple(sent):
        drain(slot)
    for copy in along + across:
        copy.wait_send()
    for copy in outs:
        copy.wait()


def solution(mesh):
    sizes = tuple(mesh.shape[name] for name in ("bx", "by", "bz"))
    vector = P(None, "bx", "by", "bz")
    scalar = P("bx", "by", "bz")

    def on_device(position, velocity, density, energy, pinned):
        def padded(*lead):
            return pltpu.VMEM(lead + (2, PX, PY, LANES), F32)

        def plain(*lead, dtype=F32):
            return pltpu.VMEM(lead + (2, N, N, LANES), dtype)

        dma = pltpu.SemaphoreType.DMA
        v3 = jax.ShapeDtypeStruct(position.shape, F32)
        v1 = jax.ShapeDtypeStruct(density.shape, F32)
        anywhere = pl.BlockSpec(memory_space=pl.ANY)

        def body(*refs):
            kernel(sizes, *refs)

        return tuple(pl.pallas_call(
            body,
            name="lagrangian_step",
            out_shape=(v3, v3, v3, v1, v1),
            in_specs=[anywhere] * 5,
            out_specs=[anywhere] * 5,
            scratch_shapes=[
                padded(2), plain(), padded(3), padded(3), padded(3), padded(3),
                plain(3), plain(3), plain(3), plain(dtype=jnp.int32), plain(), plain(), plain(3),
                padded(3), padded(3), padded(),
                pltpu.VMEM((SLOTS, 2, 2, N, 1, LANES), F32),
                pltpu.VMEM((SLOTS, 2, 2, N, 1, LANES), F32),
                pltpu.VMEM((SLOTS, N, LANES), F32),
                pltpu.VMEM((SLOTS, 2, N, LANES), F32),
                pltpu.VMEM((EDGES, 2, 1, LANES), F32),
                pltpu.VMEM((EDGES, N, LANES), F32),
                pltpu.VMEM((EDGES, 8, LANES), F32),
                pltpu.VMEM((EDGES, 8, LANES), F32),
                pltpu.VMEM((EDGES, PY, LANES), F32),
                pltpu.VMEM((2, 2, 2, 40, LANES), F32),
                pltpu.VMEM((16, LANES), F32),
                pltpu.VMEM((sizes[2], 1, LANES), F32),
                pltpu.VMEM((sizes[0] * sizes[1], 1, LANES), F32),
                dma((5, 2)), dma((11, 2)),
                dma((SLOTS, 6)), dma((SLOTS, 6)), dma((EDGES, 4)), dma((EDGES, 4)),
                dma((sizes[2],)), dma((sizes[2],)),
                dma((sizes[0] * sizes[1],)), dma((sizes[0] * sizes[1],)),
            ],
            compiler_params=pltpu.CompilerParams(
                collective_id=0, has_side_effects=True, vmem_limit_bytes=66 * 1000 * 1000),
        )(position, velocity, density, energy, pinned))

    return jax.shard_map(
        on_device,
        mesh=mesh,
        in_specs=(vector, vector, scalar, scalar, scalar),
        out_specs=(vector, vector, vector, scalar, scalar),
        check_vma=False,
    )
```

```python
import jax
import jax.numpy as jnp
from jax import lax
from jax.experimental import pallas as pl
from jax.experimental.pallas import tpu as pltpu
from jax.sharding import PartitionSpec as P

MESH = pl.DeviceIdType.MESH
F32 = jnp.float32
N = 32
LANES = 128
PX = N + 2
PY = 48
ROWS = pl.ds(8, N)
BELOW = pl.ds(7, N)
ABOVE = pl.ds(9, N)

S_P, S_RHO, S_W, S_R, S_Q, S_ONE, S_TWO, S_VEL, S_SH, S_DE = 0, 1, 2, 5, 8, 11, 14, 17, 20, 23
SLOTS = 24
E_P, E_RHO, E_VEL, E_SH = 0, 1, 2, 5
EDGES = 8


def _lane():
    return lax.broadcasted_iota(jnp.int32, (N, LANES), 1)


def planes(body, init=0, trip=4, start=0, stop=N):
    def run(i, carry):
        return body([i * trip + j for j in range(trip)], carry)
    return lax.fori_loop(start // trip, stop // trip, run, init)


def z_below(a, b, halo):
    ra, rb = pltpu.roll(a, 1, 1), pltpu.roll(b, 1, 1)
    return jnp.where(_lane() == 0, halo, ra), jnp.where(_lane() == 0, ra, rb)


def z_above(a, b, halo):
    ra, rb = pltpu.roll(a, LANES - 1, 1), pltpu.roll(b, LANES - 1, 1)
    return jnp.where(_lane() == LANES - 1, rb, ra), jnp.where(_lane() == LANES - 1, halo, rb)


def to_ends(z, i):
    return pltpu.roll(z, LANES - 1 - 2 * i, 1)


def to_last(z, i):
    return pltpu.roll(z, LANES - 1 - 2 * i, 1)


def to_first(z, i):
    return pltpu.roll(z, LANES - 1 - 2 * i, 1)


def kernel(
    sizes,
    pos_in, vel_in, rho_in, en_in, pin_in,
    vel, acc, relaxed, sh, de, rho_f, tab,
    pres, en, w, r, q, nw, nr, nq, pin, free, mass, one, two,
    ys, yr, zs, zr, exy, exz, eyz, exyz, ze, mom, ar1, ar2,
    in_sem, face_s, face_r, edge_s, edge_r, a1s, a1r, a2s, a2r,
):
    names = ("bx", "by", "bz")
    here = [lax.axis_index(name) for name in names]

    def exists(step):
        ok = None
        for i in range(3):
            if step[i] == 0:
                continue
            one_ok = here[i] + step[i] >= 0 if step[i] < 0 else here[i] + step[i] < sizes[i]
            ok = one_ok if ok is None else jnp.logical_and(ok, one_ok)
        return ok

    def device(step):
        return tuple(lax.rem(here[i] + step[i] + sizes[i], sizes[i]) for i in range(3))

    def flag(step):
        return exists(step).astype(jnp.int32) > 0

    def neg(step):
        return tuple(-s for s in step)

    steps = ((-1, 0, 0), (1, 0, 0), (0, -1, 0), (0, 1, 0), (0, 0, -1), (0, 0, 1))
    lane = lax.broadcasted_iota(jnp.int32, (N, LANES), 1)

    def face_copy(slot, field, d):
        if d < 2:
            src, dst = ((1, PX - 1), (N, 0))[d]
            src, dst = field.at[:, src, ROWS, :], field.at[:, dst, ROWS, :]
        elif d < 4:
            src, dst = ys.at[slot, d - 2], yr.at[slot, 3 - d]
        else:
            src, dst = zs.at[slot], zr.at[slot, 5 - d]
        return pltpu.make_async_remote_copy(
            src_ref=src, dst_ref=dst, send_sem=face_s.at[slot, d], recv_sem=face_r.at[slot, d],
            device_id=device(steps[d]), device_id_type=MESH)

    def edge_copies(slot, eslot, sign):
        side = 1 if sign > 0 else 0
        row = N - 1 if sign > 0 else 0
        tile = pl.ds(N - 8, 8) if sign > 0 else pl.ds(0, 8)
        pieces = (
            ((sign, sign, 0), ys.at[slot, side, :, row], exy.at[eslot]),
            ((sign, 0, sign), zs.at[slot], exz.at[eslot]),
            ((0, sign, sign), zs.at[slot, tile], eyz.at[eslot]),
            ((sign, sign, sign), zs.at[slot, tile], exyz.at[eslot]),
        )
        return [
            (step, pltpu.make_async_remote_copy(
                src_ref=src, dst_ref=dst, send_sem=edge_s.at[eslot, i], recv_sem=edge_r.at[eslot, i],
                device_id=device(step), device_id_type=MESH))
            for i, (step, src, dst) in enumerate(pieces)
        ]

    sent = {}

    def drain(slot):
        for step, copy in sent.pop(slot):
            pl.when(exists(step))(copy.wait_send)

    def send_faces(slot, field, ds=(0, 1, 2, 3, 4, 5)):
        for d in ds:
            copy = face_copy(slot, field, d)
            pl.when(exists(steps[d]))(copy.start)
            sent.setdefault(slot, []).append((steps[d], copy))

    def send_edges(slot, eslot, sign):
        for step, copy in edge_copies(slot, eslot, sign):
            pl.when(exists(step))(copy.start)
            sent.setdefault(slot, []).append((step, copy))

    def wait_faces(slot, field, ds=(0, 1, 2, 3, 4, 5)):
        for d in ds:
            pl.when(exists(neg(steps[d])))(face_copy(slot, field, d).wait_recv)

    def wait_edges(slot, eslot, sign):
        for step, copy in edge_copies(slot, eslot, sign):
            pl.when(exists(neg(step)))(copy.wait_recv)

    zero_plane = jnp.zeros((N, LANES), F32)
    odd = lane % 2 == 1
    left = lane < LANES // 2

    def lagging(xs):
        back = jnp.minimum(xs[0], len(xs))
        return [x - back for x in xs]

    def pack_planes(slot, field, xs):
        mixed = [
            pltpu.roll(jnp.where(left, field[0, x + 1, ROWS, :], field[1, x + 1, ROWS, :]), 2 * x + 3, 1)
            for x in xs
        ]
        z = zs[slot]
        for x, m in zip(xs, mixed):
            z = jnp.where((lane >> 1) == x + 1, m, z)
        zs[slot] = z

    def pack_last(slot, field, trip=4):
        pack_planes(slot, field, list(range(N - trip, N)))

    def pack_rows(slot, h, x, v, sides=(0, 1)):
        if 0 in sides:
            ys[slot, 0, h, x] = v[0:1]
        if 1 in sides:
            ys[slot, 1, h, x] = v[N - 1:N]

    def pack(slot, field, sides=(0, 1)):
        def body(xs, carry):
            pack_planes(slot, field, xs)
            for x in xs:
                for h in range(2):
                    for s in sides:
                        row = 8 if s == 0 else 7 + N
                        ys[slot, s, h, x] = field[h, x + 1, row:row + 1, :]
            return carry
        planes(body, 0, 8)

    def unpack_rows(slot, field, sides=(0, 1)):
        have = [flag((0, -1, 0)), flag((0, 1, 0))]

        def body(x, _):
            for s in sides:
                row = 7 if s == 0 else 8 + N
                for h in range(2):
                    got = yr[slot, s, h, x]
                    field[h, x + 1, row:row + 1, :] = jnp.where(have[s], got, jnp.zeros_like(got))
            return 0
        lax.fori_loop(0, N, body, 0, unroll=4)

    def z_halo(slot, side):
        have = flag((0, 0, -1 if side == 0 else 1))
        return jnp.where(have, pltpu.roll(zr[slot, side], 1 if side == 0 else LANES - 1, 1), zero_plane)

    def z_halos(slot):
        return jnp.where(odd, z_halo(slot, 0), z_halo(slot, 1))

    def edge_halo(slot, eslot, field, sign):
        side = 0 if sign > 0 else 1
        unpack_rows(slot, field, (side,))
        step = -sign
        plane, row = (0, 7) if sign > 0 else (PX - 1, 8 + N)
        have = flag((step, step, 0))
        for h in range(2):
            got = exy[eslot, h]
            field[h, plane, row:row + 1, :] = jnp.where(have, got, jnp.zeros_like(got))
        turn, at = (LANES // 2 + 1, 1) if sign > 0 else (2 * N - 1, 2 * N + 2)
        whole = 1 if sign > 0 else LANES - 1
        beside = jnp.where(flag((step, 0, step)), exz[eslot], zero_plane)
        ze[eslot, ROWS, :] = jnp.where(lane == at, pltpu.roll(beside, turn, 1), z_halo(slot, side))
        tile_lane = lax.broadcasted_iota(jnp.int32, (8, LANES), 1)
        zero_tile = jnp.zeros((8, LANES), F32)
        corner = jnp.where(flag((step, step, step)), exyz[eslot], zero_tile)
        across = jnp.where(flag((0, step, step)), eyz[eslot], zero_tile)
        tile = pl.ds(0, 8) if sign > 0 else pl.ds(8 + N, 8)
        ze[eslot, tile, :] = jnp.where(
            tile_lane == at, pltpu.roll(corner, turn, 1), pltpu.roll(across, whole, 1))

    def clear_missing(field, planes=(0, PX - 1)):
        for plane in planes:
            step = (-1, 0, 0) if plane == 0 else (1, 0, 0)

            @pl.when(jnp.logical_not(exists(step)))
            def _():
                for h in range(2):
                    field[h, plane, ROWS, :] = zero_plane

    def neighbours(field, xs, ends):
        rolled = []
        for x in xs:
            a, b = field[0, x + 1, ROWS, :], field[1, x + 1, ROWS, :]
            end = to_ends(ends, x + 1)
            rolled.append((z_below(a, b, end), z_above(a, b, end)))
        out = []
        for x, (m, p) in zip(xs, rolled):
            i = x + 1
            centre = [field[h, i, ROWS, :] for h in range(2)]
            near = []
            for h in range(2):
                s = (field[h, i - 1, ROWS, :] + field[h, i + 1, ROWS, :]) + (
                    field[h, i, BELOW, :] + field[h, i, ABOVE, :])
                near.append(s + (m[h] + p[h]))
            out.append((x, centre, near))
        return out

    def fold(v):
        return (v[0:8] + v[8:16]) + (v[16:24] + v[24:32])

    def halves(k):
        return pl.ds(k * LANES, LANES)

    loads = {}
    for h in range(2):
        loads["rho", h] = pltpu.make_async_copy(
            rho_in.at[:, :, halves(h)], rho_f.at[h, pl.ds(1, N), ROWS, :], in_sem.at[0, h])
        loads["en", h] = pltpu.make_async_copy(en_in.at[:, :, halves(h)], en.at[h], in_sem.at[1, h])
        loads["vel", h] = pltpu.make_async_copy(
            vel_in.at[:, :, :, halves(h)], vel.at[:, h, pl.ds(1, N), ROWS, :], in_sem.at[2, h])
        loads["pos", h] = pltpu.make_async_copy(
            pos_in.at[:, :, :, halves(h)], w.at[:, h, pl.ds(1, N), ROWS, :], in_sem.at[3, h])
        loads["pin", h] = pltpu.make_async_copy(pin_in.at[:, :, halves(h)], pin.at[h], in_sem.at[4, h])
    for name in ("rho", "en", "vel", "pos", "pin"):
        for h in range(2):
            loads[name, h].start()

    clear_missing(pres, (0,))
    clear_missing(rho_f)
    clear_missing(de)
    for c in range(3):
        for field in (w, r, q, one, two):
            clear_missing(field.at[c])
        for field in (vel, sh):
            clear_missing(field.at[c], (PX - 1,))

    barrier = pltpu.get_barrier_semaphore()
    around = [s for s in ((i, j, k) for i in (0, 1) for j in (0, 1) for k in (0, 1)) if any(s)]
    around = around + [neg(s) for s in around]
    count = 0
    for step in around:
        @pl.when(exists(step))
        def _():
            pl.semaphore_signal(barrier, inc=1, device_id=device(step), device_id_type=MESH)
        count = count + exists(step).astype(jnp.int32)
    nz, nxy = sizes[2], sizes[0] * sizes[1]

    def z_peer(k):
        return (here[0], here[1], lax.rem(here[2] + k, nz))

    def xy_peer(k):
        return (lax.rem(here[0] + k // sizes[1], sizes[0]), lax.rem(here[1] + k % sizes[1], sizes[1]), here[2])

    for k in range(1, nz):
        pl.semaphore_signal(barrier, inc=1, device_id=z_peer(k), device_id_type=MESH)
    for k in range(1, nxy):
        pl.semaphore_signal(barrier, inc=1, device_id=xy_peer(k), device_id_type=MESH)

    for name in ("rho", "en"):
        for h in range(2):
            loads[name, h].wait()

    def pressure_body(xs, carry):
        back = lagging(xs)
        pack_planes(S_P, pres, back)
        pack_planes(S_RHO, rho_f, xs)
        for x in xs:
            for h in range(2):
                rho = rho_f[h, x + 1, ROWS, :]
                p = 0.1 * rho * en[h, x]
                pres[h, x + 1, ROWS, :] = p
                pack_rows(S_P, h, x, p, (1,))
                pack_rows(S_RHO, h, x, rho)
        return carry

    planes(pressure_body)
    pack_last(S_P, pres)

    pl.semaphore_wait(barrier, count + (nz - 1) + (nxy - 1))
    send_edges(S_P, E_P, 1)
    send_edges(S_RHO, E_RHO, 1)
    send_faces(S_P, pres, (5, 3, 1))
    send_faces(S_RHO, rho_f, (5, 3, 1, 4, 2, 0))

    for name in ("vel", "pos", "pin"):
        for h in range(2):
            loads[name, h].wait()

    def advance(c):
        def body(xs, carry):
            pack_planes(S_W + c, w.at[c], lagging(xs))
            for x in xs:
                for h in range(2):
                    v = w[c, h, x + 1, ROWS, :] + 0.6 * vel[c, h, x + 1, ROWS, :]
                    w[c, h, x + 1, ROWS, :] = v
                    pack_rows(S_W + c, h, x, v)
            return carry
        planes(body)
        pack_last(S_W + c, w.at[c])
        send_faces(S_W + c, w.at[c])

    for c in range(3):
        advance(c)

    def mask_body(x, _):
        for h in range(2):
            free[h, x] = 0.8 - 0.8 * pin[h, x].astype(F32)
        return 0
    lax.fori_loop(0, N, mask_body, 0)

    wait_faces(S_P, pres, (5, 3, 1))
    wait_edges(S_P, E_P, 1)
    wait_faces(S_RHO, rho_f)
    wait_edges(S_RHO, E_RHO, 1)
    edge_halo(S_P, E_P, pres, 1)
    edge_halo(S_RHO, E_RHO, rho_f, 1)
    unpack_rows(S_RHO, rho_f, (1,))
    zay = ze[E_P, ROWS, :] + ze[E_P, BELOW, :]
    zdy = ze[E_P, BELOW, :] - ze[E_P, ROWS, :]
    zrho = ze[E_RHO, ROWS, :] + ze[E_RHO, BELOW, :]

    def force_terms(i):
        ay, dy = [], []
        for h in range(2):
            c, b = pres[h, i, ROWS, :], pres[h, i, BELOW, :]
            ay.append(c + b)
            dy.append(b - c)
        aym = z_below(ay[0], ay[1], to_first(zay, i))
        dym = z_below(dy[0], dy[1], to_first(zdy, i))
        return tuple(
            t for h in range(2) for t in (ay[h] + aym[h], dy[h] + dym[h], aym[h] - ay[h]))

    def force_body(i, before):
        terms = [before] + [force_terms(4 * i + j + 1) for j in range(4)]
        for j in range(4):
            old, now = terms[j], terms[j + 1]
            for h in range(2):
                r[0, h, 4 * i + j + 1, ROWS, :] = old[3 * h] - now[3 * h]
                r[1, h, 4 * i + j + 1, ROWS, :] = old[3 * h + 1] + now[3 * h + 1]
                r[2, h, 4 * i + j + 1, ROWS, :] = old[3 * h + 2] + now[3 * h + 2]
        return terms[4]
    lax.fori_loop(0, N // 4, force_body, force_terms(0))

    for c in range(3):
        pack(S_R + c, r.at[c])
        send_faces(S_R + c, r.at[c])

    def mass_terms(i):
        ay = [rho_f[h, i, ROWS, :] + rho_f[h, i, BELOW, :] for h in range(2)]
        aym = z_below(ay[0], ay[1], to_first(zrho, i))
        return ay[0] + aym[0], ay[1] + aym[1]

    def mass_body(i, before):
        terms = [before] + [mass_terms(4 * i + j + 1) for j in range(4)]
        for j in range(4):
            for h in range(2):
                mass[h, 4 * i + j] = 0.125 * (terms[j][h] + terms[j + 1][h]) + 1.2
        return terms[4]
    lax.fori_loop(0, N // 4, mass_body, mass_terms(0))

    zero_tile = jnp.zeros((8, LANES), F32)

    def receive(slot, field):
        wait_faces(slot, field)
        unpack_rows(slot, field)
        return z_halos(slot)

    for c in range(3):
        ends = receive(S_R + c, r.at[c])

        def image_body(xs, carry, c=c, ends=ends):
            m0, m1, m2 = carry
            pack_planes(S_Q + c, q.at[c], lagging(xs))
            for x, centre, near in neighbours(r.at[c], xs, ends):
                for h in range(2):
                    image = mass[h, x] * centre[h] + 0.2 * near[h]
                    q[c, h, x + 1, ROWS, :] = image
                    nr[c, h, x] = near[h]
                    m0 = m0 + fold(centre[h] * centre[h])
                    m1 = m1 + fold(centre[h] * image)
                    m2 = m2 + fold(image * image)
                    pack_rows(S_Q + c, h, x, image)
            return m0, m1, m2
        moments = planes(image_body, (zero_tile, zero_tile, zero_tile))
        pack_last(S_Q + c, q.at[c])
        send_faces(S_Q + c, q.at[c])
        for k, m in enumerate(moments):
            mom[4 * c + k:4 * c + k + 1, :] = jnp.sum(m, axis=0, keepdims=True)

    def near_w(c):
        ends = receive(S_W + c, w.at[c])

        def body(xs, carry):
            for x, _centre, near in neighbours(w.at[c], xs, ends):
                for h in range(2):
                    nw[c, h, x] = near[h]
            return carry
        planes(body)

    near_w(0)
    for c in range(3):
        ends = receive(S_Q + c, q.at[c])

        def second_body(xs, m3, c=c, ends=ends):
            for x, centre, near in neighbours(q.at[c], xs, ends):
                for h in range(2):
                    nq[c, h, x] = near[h]
                    m3 = m3 + fold(centre[h] * (mass[h, x] * centre[h] + 0.2 * near[h]))
            return m3
        m3 = planes(second_body, zero_tile)
        mom[4 * c + 3:4 * c + 4, :] = jnp.sum(m3, axis=0, keepdims=True)
    mom[12:16, :] = jnp.zeros((4, LANES), F32)

    total = jnp.sum(mom[...], axis=1, keepdims=True)
    on_row = lax.broadcasted_iota(jnp.int32, (16, LANES), 0)
    on_lane = lax.broadcasted_iota(jnp.int32, (16, LANES), 1)
    ar1[0] = jnp.sum(jnp.where(on_row == on_lane, total, 0.0), axis=0, keepdims=True)

    def reduce_copies(buf, send, recv, peer, peers):
        return [
            pltpu.make_async_remote_copy(
                src_ref=buf.at[0], dst_ref=buf.at[k], send_sem=send.at[k], recv_sem=recv.at[k],
                device_id=peer(k), device_id_type=MESH)
            for k in range(1, peers)
        ]

    def gathered(buf, copies):
        for copy in copies:
            copy.wait_recv()
        parts = [buf[k] for k in range(len(copies) + 1)]
        while len(parts) > 1:
            parts = [a + b for a, b in zip(parts[::2], parts[1::2])]
        return parts[0]

    along = reduce_copies(ar1, a1s, a1r, z_peer, nz)
    for copy in along:
        copy.start()
    near_w(1)
    ar2[0] = gathered(ar1, along)
    across = reduce_copies(ar2, a2s, a2r, xy_peer, nxy)
    for copy in across:
        copy.start()
    near_w(2)
    sums = gathered(ar2, across)
    row_lane = lax.broadcasted_iota(jnp.int32, (1, LANES), 1)

    def pick(k):
        return jnp.sum(jnp.where(row_lane == k, sums, 0.0), axis=1, keepdims=True)

    for c in range(3):
        m0, m1, m2, m3 = [pick(4 * c + k) for k in range(4)]
        a1 = m0 / m1
        new = m0 - 2.0 * a1 * m1 + a1 * a1 * m2
        b1 = 1.0 + new / m0
        a2 = new / (b1 * b1 * m1 - 2.0 * a1 * b1 * m2 + a1 * a1 * m3)
        c1 = jnp.broadcast_to(a1 + a2 * b1, (N, LANES))
        c2 = jnp.broadcast_to(-a1 * a2, (N, LANES))

        def step_body(xs, carry, c=c, c1=c1, c2=c2):
            pack_planes(S_ONE + c, one.at[c], lagging(xs))
            for x in xs:
                i = x + 1
                for h in range(2):
                    a = c1 * r[c, h, i, ROWS, :] + c2 * q[c, h, i, ROWS, :]
                    acc[c, h, x] = a
                    v = vel[c, h, i, ROWS, :] + 0.6 * a
                    vel[c, h, i, ROWS, :] = v
                    moved = w[c, h, i, ROWS, :] + 0.36 * a
                    w[c, h, i, ROWS, :] = moved
                    near = nw[c, h, x] + 0.36 * (c1 * nr[c, h, x] + c2 * nq[c, h, x])
                    u = moved + free[h, x] * (near * (1.0 / 6.0) - moved)
                    one[c, h, i, ROWS, :] = u
                    pack_rows(S_ONE + c, h, x, u)
            return carry
        drain(S_W + c)
        planes(step_body)
        pack_last(S_ONE + c, one.at[c])
        send_faces(S_ONE + c, one.at[c])
    for c in range(3):
        pack(S_VEL + c, vel.at[c], (0,))
        send_faces(S_VEL + c, vel.at[c], (0, 2, 4))
        send_edges(S_VEL + c, E_VEL + c, -1)

    def swept(field, c, xs, ends):
        return [
            (x, [centre[h] + free[h, x] * (near[h] * (1.0 / 6.0) - centre[h]) for h in range(2)])
            for x, centre, near in neighbours(field.at[c], xs, ends)
        ]

    for c in range(3):
        ends = receive(S_ONE + c, one.at[c])

        def sweep_body(xs, carry, c=c, ends=ends):
            pack_planes(S_TWO + c, two.at[c], lagging(xs))
            for x, u in swept(one, c, xs, ends):
                for h in range(2):
                    two[c, h, x + 1, ROWS, :] = u[h]
                    pack_rows(S_TWO + c, h, x, u[h])
            return carry
        planes(sweep_body)
        pack_last(S_TWO + c, two.at[c])
        send_faces(S_TWO + c, two.at[c])

    for c in range(3):
        wait_faces(S_VEL + c, vel.at[c], (0, 2, 4))
        wait_edges(S_VEL + c, E_VEL + c, -1)
        edge_halo(S_VEL + c, E_VEL + c, vel.at[c], -1)

    def rows_up(k):
        return ze[k, ROWS, :], ze[k, ABOVE, :]

    zx, zy, zz3 = rows_up(E_VEL), rows_up(E_VEL + 1), rows_up(E_VEL + 2)
    z_s1 = (zy[1] - zy[0]) + (zz3[0] + zz3[1])
    z_s2 = zx[0] + zx[1]

    def div_terms(i):
        s1, s2, s3 = [], [], []
        for h in range(2):
            ax = vel[0, h, i, ROWS, :] + vel[0, h, i, ABOVE, :]
            dy = vel[1, h, i, ABOVE, :] - vel[1, h, i, ROWS, :]
            az = vel[2, h, i, ROWS, :] + vel[2, h, i, ABOVE, :]
            s1.append(dy + az)
            s2.append(ax)
            s3.append(dy - az)
        u1 = z_above(s1[0], s1[1], to_last(z_s1, i))
        u2 = z_above(s2[0], s2[1], to_last(z_s2, i))
        plus, minus = [], []
        for h in range(2):
            flat, along_x = s3[h] + u1[h], s2[h] + u2[h]
            plus.append(flat + along_x)
            minus.append(flat - along_x)
        return plus, minus

    def div_body(k, before):
        back = jnp.maximum(2 * k - 2, 0)
        pack_planes(S_DE, de, [back, back + 1])
        for j in range(2):
            x = 2 * k + j
            plus, minus = div_terms(x + 2)
            for h in range(2):
                spread = before[h] + plus[h]
                value = rho_f[h, x + 1, ROWS, :] * (en[h, x] * (1.0 - 0.06 * spread))
                de[h, x + 1, ROWS, :] = value
                pack_rows(S_DE, h, x, value)
            before = minus
        return tuple(before)
    lax.fori_loop(0, N // 2, div_body, tuple(div_terms(1)[1]))
    pack_last(S_DE, de, 2)
    send_faces(S_DE, de)

    for c in range(3):
        ends = receive(S_TWO + c, two.at[c])

        def last_body(xs, carry, c=c, ends=ends):
            pack_planes(S_SH + c, sh.at[c], lagging(xs))
            for x, u in swept(two, c, xs, ends):
                for h in range(2):
                    relaxed[c, h, x] = u[h]
                    s = u[h] - w[c, h, x + 1, ROWS, :]
                    sh[c, h, x + 1, ROWS, :] = s
                    pack_rows(S_SH + c, h, x, s, (0,))
            return carry
        planes(last_body)
        pack_last(S_SH + c, sh.at[c])
        send_faces(S_SH + c, sh.at[c], (4, 2, 0))
        send_edges(S_SH + c, E_SH + c, -1)

    receive(S_DE, de)
    for c in range(3):
        wait_faces(S_SH + c, sh.at[c], (4, 2, 0))
        wait_edges(S_SH + c, E_SH + c, -1)
        edge_halo(S_SH + c, E_SH + c, sh.at[c], -1)
    zx, zz3 = rows_up(E_SH), rows_up(E_SH + 2)
    tab[0, 0:N, :] = zx[0] + zx[1]
    z_y = ze[E_SH + 1, pl.ds(8, 40), :]
    tab[1] = z_y + pltpu.roll(z_y, LANES - 2, 1)
    z_z = zz3[0] + zz3[1]
    z_z = 0.25 * (z_z + pltpu.roll(z_z, LANES - 2, 1))
    for f, slot in enumerate((S_RHO, S_DE)):
        tab[2 + f, 0:N, :] = jnp.where(
            odd, z_halo(slot, 0), z_z * jnp.where(z_z > 0, z_halo(slot, 1), zs[slot]))

    for slot in tuple(sent):
        drain(slot)
    for copy in along + across:
        copy.wait_send()


def remap(
    vel, acc, relaxed, sh, de, rho_f, tab,
    v_out, a_out, r_out, d_out, e_out,
    nr, gy, out_sem,
):
    fields = (rho_f, de)
    wide = pl.ds(8, 40)
    outs = []

    def halves(k):
        return pl.ds(k * LANES, LANES)

    def write(src, dst, i, h):
        copy = pltpu.make_async_copy(src, dst, out_sem.at[i, h])
        copy.start()
        outs.append(copy)

    for c in range(3):
        for h in range(2):
            write(acc.at[c, h], a_out.at[c, :, :, halves(h)], c, h)
            write(vel.at[c, h, pl.ds(1, N), ROWS, :], v_out.at[c, :, :, halves(h)], 3 + c, h)
            write(relaxed.at[c, h], r_out.at[c, :, :, halves(h)], 6 + c, h)
    wide_last = lax.broadcasted_iota(jnp.int32, (40, LANES), 1) == LANES - 1

    def flux_x(i):
        a = [sh[0, h, i, ROWS, :] + sh[0, h, i, ABOVE, :] for h in range(2)]
        up = z_above(a[0], a[1], to_last(tab[0, 0:N, :], i))
        out = []
        for h in range(2):
            s = 0.25 * (a[h] + up[h])
            for field in fields:
                out.append(s * jnp.where(s > 0, field[h, i, ROWS, :], field[h, i - 1, ROWS, :]))
        return tuple(out)

    def remap_x(k, before):
        for j in range(2):
            x = 2 * k + j
            now = flux_x(x + 2)
            for h in range(2):
                for f, field in enumerate(fields):
                    nr[f, h, x] = field[h, x + 1, ROWS, :] + (now[2 * h + f] - before[2 * h + f])
            before = now
        return before
    lax.fori_loop(0, N // 2, remap_x, flux_x(1))

    def remap_y(xs, carry):
        for j, x in enumerate(xs):
            i = x + 1
            t = [sh[1, h, i, wide, :] + sh[1, h, i + 1, wide, :] for h in range(2)]
            ra, rb = [pltpu.roll(v, LANES - 1, 1) for v in t]
            up = (jnp.where(wide_last, rb, ra), jnp.where(wide_last, to_last(tab[1], i), rb))
            for h in range(2):
                s = 0.25 * (t[h] + up[h])
                for f, field in enumerate(fields):
                    gy[j, f, h] = s * jnp.where(s > 0, field[h, i, wide, :], field[h, i, pl.ds(7, 40), :])
        for j, x in enumerate(xs):
            for h in range(2):
                for f in range(2):
                    nr[f, h, x] = nr[f, h, x] + (gy[j, f, h, 1:N + 1, :] - gy[j, f, h, 0:N, :])
        return carry
    planes(remap_y, 0, 2)

    def remap_z(xs, carry):
        for x in xs:
            i = x + 1
            s = [
                0.25 * ((sh[2, h, i, ROWS, :] + sh[2, h, i, ABOVE, :])
                        + (sh[2, h, i + 1, ROWS, :] + sh[2, h, i + 1, ABOVE, :]))
                for h in range(2)
            ]
            for f, field in enumerate(fields):
                own = [field[h, i, ROWS, :] for h in range(2)]
                end = to_ends(tab[2 + f, 0:N, :], i)
                under = z_below(own[0], own[1], end)
                g = [s[h] * jnp.where(s[h] > 0, own[h], under[h]) for h in range(2)]
                over = z_above(g[0], g[1], end)
                for h in range(2):
                    nr[f, h, x] = nr[f, h, x] + (over[h] - g[h])
        return carry
    for part in range(4):
        lo = 8 * part
        planes(remap_z, 0, 2, lo, lo + 8)
        for f, out in enumerate((d_out, e_out)):
            for h in range(2):
                write(nr.at[f, h, pl.ds(lo, 8)], out.at[pl.ds(lo, 8), :, halves(h)], 9 + 4 * f + part, h)
    for copy in outs:
        copy.wait()


def solution(mesh):
    sizes = tuple(mesh.shape[name] for name in ("bx", "by", "bz"))
    vector = P(None, "bx", "by", "bz")
    scalar = P("bx", "by", "bz")

    def on_device(position, velocity, density, energy, pinned):
        def padded(*lead):
            return pltpu.VMEM(lead + (2, PX, PY, LANES), F32)

        def plain(*lead, dtype=F32):
            return pltpu.VMEM(lead + (2, N, N, LANES), dtype)

        dma = pltpu.SemaphoreType.DMA
        v3 = jax.ShapeDtypeStruct(position.shape, F32)
        v1 = jax.ShapeDtypeStruct(density.shape, F32)
        anywhere = pl.BlockSpec(memory_space=pl.ANY)

        def body(*refs):
            kernel(sizes, *refs)

        in_vmem = pl.BlockSpec(memory_space=pltpu.VMEM)
        handed = pl.pallas_call(
            body,
            name="lagrangian_step",
            out_shape=(
                padded(3), plain(3), plain(3), padded(3), padded(), padded(), pltpu.VMEM((4, 40, LANES), F32)),
            in_specs=[anywhere] * 5,
            out_specs=[in_vmem] * 7,
            scratch_shapes=[
                padded(), plain(), padded(3), padded(3), padded(3),
                plain(3), plain(3), plain(3), plain(dtype=jnp.int32), plain(), plain(),
                padded(3), padded(3),
                pltpu.VMEM((SLOTS, 2, 2, N, 1, LANES), F32),
                pltpu.VMEM((SLOTS, 2, 2, N, 1, LANES), F32),
                pltpu.VMEM((SLOTS, N, LANES), F32),
                pltpu.VMEM((SLOTS, 2, N, LANES), F32),
                pltpu.VMEM((EDGES, 2, 1, LANES), F32),
                pltpu.VMEM((EDGES, N, LANES), F32),
                pltpu.VMEM((EDGES, 8, LANES), F32),
                pltpu.VMEM((EDGES, 8, LANES), F32),
                pltpu.VMEM((EDGES, PY, LANES), F32),
                pltpu.VMEM((16, LANES), F32),
                pltpu.VMEM((sizes[2], 1, LANES), F32),
                pltpu.VMEM((sizes[0] * sizes[1], 1, LANES), F32),
                dma((5, 2)),
                dma((SLOTS, 6)), dma((SLOTS, 6)), dma((EDGES, 4)), dma((EDGES, 4)),
                dma((sizes[2],)), dma((sizes[2],)),
                dma((sizes[0] * sizes[1],)), dma((sizes[0] * sizes[1],)),
            ],
            compiler_params=pltpu.CompilerParams(
                collective_id=0, has_side_effects=True, vmem_limit_bytes=46 * 1000 * 1000),
        )(position, velocity, density, energy, pinned)
        return tuple(pl.pallas_call(
            remap,
            name="remap",
            out_shape=(v3, v3, v3, v1, v1),
            in_specs=[in_vmem] * 7,
            out_specs=[anywhere] * 5,
            scratch_shapes=[plain(2), pltpu.VMEM((2, 2, 2, 40, LANES), F32), dma((17, 2))],
            compiler_params=pltpu.CompilerParams(vmem_limit_bytes=8 * 1000 * 1000),
        )(*handed))

    return jax.shard_map(
        on_device,
        mesh=mesh,
        in_specs=(vector, vector, scalar, scalar, scalar),
        out_specs=(vector, vector, vector, scalar, scalar),
        check_vma=False,
    )
```

```python
import jax
import jax.numpy as jnp
from jax import lax
from jax.experimental import pallas as pl
from jax.experimental.pallas import tpu as pltpu
from jax.sharding import PartitionSpec as P

MESH = pl.DeviceIdType.MESH
F32 = jnp.float32
N = 32
LANES = 128
PX = N + 2
PY = 48
TRIP = 16
ROWS = pl.ds(8, N)
BELOW = pl.ds(7, N)
ABOVE = pl.ds(9, N)

S_P, S_RHO, S_W, S_R, S_Q, S_ONE, S_TWO, S_VEL, S_SH, S_DE = 0, 1, 2, 5, 8, 11, 14, 17, 20, 23
SLOTS = 24
E_P, E_RHO, E_VEL, E_SH = 0, 1, 2, 5
EDGES = 8


def _lane():
    return lax.broadcasted_iota(jnp.int32, (N, LANES), 1)


def planes(body, init=0, trip=TRIP, start=0, stop=N):
    def run(i, carry):
        return body([i * trip + j for j in range(trip)], carry)
    return lax.fori_loop(start // trip, stop // trip, run, init)


def z_below(a, b, halo):
    ra, rb = pltpu.roll(a, 1, 1), pltpu.roll(b, 1, 1)
    return jnp.where(_lane() == 0, halo, ra), jnp.where(_lane() == 0, ra, rb)


def z_above(a, b, halo):
    ra, rb = pltpu.roll(a, LANES - 1, 1), pltpu.roll(b, LANES - 1, 1)
    return jnp.where(_lane() == LANES - 1, rb, ra), jnp.where(_lane() == LANES - 1, halo, rb)


def to_ends(z, i):
    return pltpu.roll(z, LANES - 1 - 2 * i, 1)


def to_last(z, i):
    return pltpu.roll(z, LANES - 1 - 2 * i, 1)


def to_first(z, i):
    return pltpu.roll(z, LANES - 1 - 2 * i, 1)


def kernel(
    sizes,
    pos_in, vel_in, rho_in, en_in, pin_in,
    vel, acc, relaxed, sh, de, rho_f, tab, partial,
    pres, en, w, r, q, nw, nr, nq, pin, free, mass, one,
    ys, yr, zs, zr, exy, exz, eyz, exyz, ze, band, gy, mom, ar1, ar2,
    in_sem, face_s, face_r, edge_s, edge_r, a1s, a1r, a2s, a2r,
):
    names = ("bx", "by", "bz")
    here = [lax.axis_index(name) for name in names]

    def exists(step):
        ok = None
        for i in range(3):
            if step[i] == 0:
                continue
            one_ok = here[i] + step[i] >= 0 if step[i] < 0 else here[i] + step[i] < sizes[i]
            ok = one_ok if ok is None else jnp.logical_and(ok, one_ok)
        return ok

    def device(step):
        return tuple(lax.rem(here[i] + step[i] + sizes[i], sizes[i]) for i in range(3))

    def flag(step):
        return exists(step).astype(jnp.int32) > 0

    def neg(step):
        return tuple(-s for s in step)

    steps = ((-1, 0, 0), (1, 0, 0), (0, -1, 0), (0, 1, 0), (0, 0, -1), (0, 0, 1))
    lane = lax.broadcasted_iota(jnp.int32, (N, LANES), 1)

    def some(slot, n):
        return slot if n == 1 else pl.ds(slot, n)

    def face_copy(slot, field, d, n=1):
        at = some(slot, n)
        if d < 2:
            src, dst = ((1, PX - 1), (N, 0))[d]
            lead = () if n == 1 else (slice(None),)
            src, dst = [field.at[lead + (slice(None), plane, ROWS, slice(None))] for plane in (src, dst)]
        elif d < 4:
            src, dst = ys.at[at, d - 2], yr.at[at, 3 - d]
        else:
            src, dst = zs.at[at], zr.at[at, 5 - d]
        return pltpu.make_async_remote_copy(
            src_ref=src, dst_ref=dst, send_sem=face_s.at[slot, d], recv_sem=face_r.at[slot, d],
            device_id=device(steps[d]), device_id_type=MESH)

    def edge_copies(slot, eslot, sign, n=1):
        at, to = some(slot, n), some(eslot, n)
        side = 1 if sign > 0 else 0
        row = N - 1 if sign > 0 else 0
        tile = pl.ds(N - 8, 8) if sign > 0 else pl.ds(0, 8)
        pieces = (
            ((sign, sign, 0), ys.at[at, side, :, row], exy.at[to]),
            ((sign, 0, sign), zs.at[at], exz.at[to]),
            ((0, sign, sign), zs.at[at, tile], eyz.at[to]),
            ((sign, sign, sign), zs.at[at, tile], exyz.at[to]),
        )
        return [
            (step, pltpu.make_async_remote_copy(
                src_ref=src, dst_ref=dst, send_sem=edge_s.at[eslot, i], recv_sem=edge_r.at[eslot, i],
                device_id=device(step), device_id_type=MESH))
            for i, (step, src, dst) in enumerate(pieces)
        ]

    sent = {}

    def drain(*slots):
        for slot in slots:
            for step, copy in sent.pop(slot, ()):
                pl.when(exists(step))(copy.wait_send)

    def send_faces(slot, field, ds=(0, 1, 2, 3, 4, 5), n=1):
        for d in ds:
            copy = face_copy(slot, field, d, n)
            pl.when(exists(steps[d]))(copy.start)
            sent.setdefault(slot, []).append((steps[d], copy))

    def send_edges(slot, eslot, sign, n=1):
        for step, copy in edge_copies(slot, eslot, sign, n):
            pl.when(exists(step))(copy.start)
            sent.setdefault(slot, []).append((step, copy))

    def wait_faces(slot, field, ds=(0, 1, 2, 3, 4, 5), n=1):
        for d in ds:
            pl.when(exists(neg(steps[d])))(face_copy(slot, field, d, n).wait_recv)

    def wait_edges(slot, eslot, sign, n=1):
        for step, copy in edge_copies(slot, eslot, sign, n):
            pl.when(exists(neg(step)))(copy.wait_recv)

    zero_plane = jnp.zeros((N, LANES), F32)
    odd = lane % 2 == 1
    left = lane < LANES // 2

    def lagging(xs):
        back = jnp.minimum(xs[0], len(xs))
        return [x - back for x in xs]

    def pack_planes(slot, field, xs):
        mixed = [
            pltpu.roll(jnp.where(left, field[0, x + 1, ROWS, :], field[1, x + 1, ROWS, :]), 2 * x + 3, 1)
            for x in xs
        ]
        z = zs[slot]
        for x, m in zip(xs, mixed):
            z = jnp.where((lane >> 1) == x + 1, m, z)
        zs[slot] = z

    def pack_last(slot, field, trip=TRIP):
        pack_planes(slot, field, list(range(N - trip, N)))

    def pack_rows(slot, h, x, v, sides=(0, 1)):
        if 0 in sides:
            ys[slot, 0, h, x] = v[0:1]
        if 1 in sides:
            ys[slot, 1, h, x] = v[N - 1:N]

    def pack(slot, field, sides=(0, 1)):
        def body(xs, carry):
            pack_planes(slot, field, xs)
            for x in xs:
                for h in range(2):
                    for s in sides:
                        row = 8 if s == 0 else 7 + N
                        ys[slot, s, h, x] = field[h, x + 1, row:row + 1, :]
            return carry
        planes(body, 0, 8)

    def unpack_rows(slot, field, sides=(0, 1)):
        have = [flag((0, -1, 0)), flag((0, 1, 0))]

        def body(x, _):
            for s in sides:
                row = 7 if s == 0 else 8 + N
                for h in range(2):
                    got = yr[slot, s, h, x]
                    field[h, x + 1, row:row + 1, :] = jnp.where(have[s], got, jnp.zeros_like(got))
            return 0
        lax.fori_loop(0, N, body, 0, unroll=4)

    def z_halo(slot, side):
        have = flag((0, 0, -1 if side == 0 else 1))
        return jnp.where(have, pltpu.roll(zr[slot, side], 1 if side == 0 else LANES - 1, 1), zero_plane)

    def z_halos(slot):
        return jnp.where(odd, z_halo(slot, 0), z_halo(slot, 1))

    def edge_halo(slot, eslot, field, sign):
        side = 0 if sign > 0 else 1
        unpack_rows(slot, field, (side,))
        step = -sign
        plane, row = (0, 7) if sign > 0 else (PX - 1, 8 + N)
        have = flag((step, step, 0))
        for h in range(2):
            got = exy[eslot, h]
            field[h, plane, row:row + 1, :] = jnp.where(have, got, jnp.zeros_like(got))
        turn, at = (LANES // 2 + 1, 1) if sign > 0 else (2 * N - 1, 2 * N + 2)
        whole = 1 if sign > 0 else LANES - 1
        beside = jnp.where(flag((step, 0, step)), exz[eslot], zero_plane)
        ze[eslot, ROWS, :] = jnp.where(lane == at, pltpu.roll(beside, turn, 1), z_halo(slot, side))
        tile_lane = lax.broadcasted_iota(jnp.int32, (8, LANES), 1)
        zero_tile = jnp.zeros((8, LANES), F32)
        corner = jnp.where(flag((step, step, step)), exyz[eslot], zero_tile)
        across = jnp.where(flag((0, step, step)), eyz[eslot], zero_tile)
        tile = pl.ds(0, 8) if sign > 0 else pl.ds(8 + N, 8)
        ze[eslot, tile, :] = jnp.where(
            tile_lane == at, pltpu.roll(corner, turn, 1), pltpu.roll(across, whole, 1))

    def clear_missing(field, planes=(0, PX - 1)):
        for plane in planes:
            step = (-1, 0, 0) if plane == 0 else (1, 0, 0)

            @pl.when(jnp.logical_not(exists(step)))
            def _():
                for h in range(2):
                    field[h, plane, ROWS, :] = zero_plane

    at_row = lax.broadcasted_iota(jnp.int32, (2 * LANES, 2 * LANES), 0)
    at_column = lax.broadcasted_iota(jnp.int32, (2 * LANES, 2 * LANES), 1)
    band[...] = jnp.where(jnp.abs(at_row - at_column) == 1, 1.0, 0.0).astype(jnp.bfloat16)

    def neighbours(field, xs, ends):
        both = [
            jnp.concatenate([field[h, x + 1, ROWS, :] for x in xs], axis=0) for h in range(2)
        ]
        whole = jnp.concatenate(both, axis=1)
        lead = whole.astype(jnp.bfloat16)
        rest = (whole - lead.astype(F32)).astype(jnp.bfloat16)
        along_z = jnp.dot(lead, band[...], preferred_element_type=F32) + jnp.dot(
            rest, band[...], preferred_element_type=F32)
        out = []
        for j, x in enumerate(xs):
            i = x + 1
            end = to_ends(ends, i)
            edge = (jnp.where(lane == 0, end, 0.0), jnp.where(lane == LANES - 1, end, 0.0))
            centre = [field[h, i, ROWS, :] for h in range(2)]
            near = []
            for h in range(2):
                s = (field[h, i - 1, ROWS, :] + field[h, i + 1, ROWS, :]) + (
                    field[h, i, BELOW, :] + field[h, i, ABOVE, :])
                z = along_z[N * j:N * j + N, LANES * h:LANES * h + LANES]
                near.append(s + (z + edge[h]))
            out.append((x, centre, near))
        return out

    def fold(v):
        return (v[0:8] + v[8:16]) + (v[16:24] + v[24:32])

    def halves(k):
        return pl.ds(k * LANES, LANES)

    loads = {}
    for h in range(2):
        loads["rho", h] = pltpu.make_async_copy(
            rho_in.at[:, :, halves(h)], rho_f.at[h, pl.ds(1, N), ROWS, :], in_sem.at[0, h])
        loads["en", h] = pltpu.make_async_copy(en_in.at[:, :, halves(h)], en.at[h], in_sem.at[1, h])
        loads["vel", h] = pltpu.make_async_copy(
            vel_in.at[:, :, :, halves(h)], vel.at[:, h, pl.ds(1, N), ROWS, :], in_sem.at[2, h])
        loads["pos", h] = pltpu.make_async_copy(
            pos_in.at[:, :, :, halves(h)], w.at[:, h, pl.ds(1, N), ROWS, :], in_sem.at[3, h])
        loads["pin", h] = pltpu.make_async_copy(pin_in.at[:, :, halves(h)], pin.at[h], in_sem.at[4, h])
    for name in ("rho", "en", "vel", "pos", "pin"):
        for h in range(2):
            loads[name, h].start()

    clear_missing(pres, (0,))
    clear_missing(rho_f)
    clear_missing(de)
    for c in range(3):
        for field in (w, r, q, one):
            clear_missing(field.at[c])
        for field in (vel, sh):
            clear_missing(field.at[c], (PX - 1,))

    barrier = pltpu.get_barrier_semaphore()
    around = [s for s in ((i, j, k) for i in (0, 1) for j in (0, 1) for k in (0, 1)) if any(s)]
    around = around + [neg(s) for s in around]
    count = 0
    for step in around:
        @pl.when(exists(step))
        def _():
            pl.semaphore_signal(barrier, inc=1, device_id=device(step), device_id_type=MESH)
        count = count + exists(step).astype(jnp.int32)
    nz, nxy = sizes[2], sizes[0] * sizes[1]

    def z_peer(k):
        return (here[0], here[1], lax.rem(here[2] + k, nz))

    def xy_peer(k):
        return (lax.rem(here[0] + k // sizes[1], sizes[0]), lax.rem(here[1] + k % sizes[1], sizes[1]), here[2])

    for k in range(1, nz):
        pl.semaphore_signal(barrier, inc=1, device_id=z_peer(k), device_id_type=MESH)
    for k in range(1, nxy):
        pl.semaphore_signal(barrier, inc=1, device_id=xy_peer(k), device_id_type=MESH)

    for name in ("rho", "en"):
        for h in range(2):
            loads[name, h].wait()

    def pressure_body(xs, carry):
        back = lagging(xs)
        pack_planes(S_P, pres, back)
        pack_planes(S_RHO, rho_f, xs)
        for x in xs:
            for h in range(2):
                rho = rho_f[h, x + 1, ROWS, :]
                p = 0.1 * rho * en[h, x]
                pres[h, x + 1, ROWS, :] = p
                pack_rows(S_P, h, x, p, (1,))
                pack_rows(S_RHO, h, x, rho)
        return carry

    planes(pressure_body)
    pack_last(S_P, pres)

    pl.semaphore_wait(barrier, count + (nz - 1) + (nxy - 1))
    send_edges(S_P, E_P, 1, 2)
    send_faces(S_P, None, (5, 3), 2)
    send_faces(S_P, pres, (1,))
    send_faces(S_RHO, rho_f, (1, 4, 2, 0))

    for name in ("vel", "pos", "pin"):
        for h in range(2):
            loads[name, h].wait()

    def advance(c):
        def body(xs, carry):
            pack_planes(S_W + c, w.at[c], lagging(xs))
            for x in xs:
                for h in range(2):
                    v = w[c, h, x + 1, ROWS, :] + 0.6 * vel[c, h, x + 1, ROWS, :]
                    w[c, h, x + 1, ROWS, :] = v
                    pack_rows(S_W + c, h, x, v)
            return carry
        planes(body)
        pack_last(S_W + c, w.at[c])

    for c in range(3):
        advance(c)

    wait_faces(S_P, None, (5, 3), 2)
    wait_edges(S_P, E_P, 1, 2)
    wait_faces(S_P, pres, (1,))
    wait_faces(S_RHO, rho_f, (1, 4, 2, 0))
    edge_halo(S_P, E_P, pres, 1)
    edge_halo(S_RHO, E_RHO, rho_f, 1)
    unpack_rows(S_RHO, rho_f, (1,))
    zay = ze[E_P, ROWS, :] + ze[E_P, BELOW, :]
    zdy = ze[E_P, BELOW, :] - ze[E_P, ROWS, :]
    zrho = ze[E_RHO, ROWS, :] + ze[E_RHO, BELOW, :]

    def force_terms(i):
        ay, dy = [], []
        for h in range(2):
            c, b = pres[h, i, ROWS, :], pres[h, i, BELOW, :]
            ay.append(c + b)
            dy.append(b - c)
        aym = z_below(ay[0], ay[1], to_first(zay, i))
        dym = z_below(dy[0], dy[1], to_first(zdy, i))
        return tuple(
            t for h in range(2) for t in (ay[h] + aym[h], dy[h] + dym[h], aym[h] - ay[h]))

    def force_body(i, before):
        terms = [before] + [force_terms(4 * i + j + 1) for j in range(4)]
        for j in range(4):
            old, now = terms[j], terms[j + 1]
            for h in range(2):
                r[0, h, 4 * i + j + 1, ROWS, :] = old[3 * h] - now[3 * h]
                r[1, h, 4 * i + j + 1, ROWS, :] = old[3 * h + 1] + now[3 * h + 1]
                r[2, h, 4 * i + j + 1, ROWS, :] = old[3 * h + 2] + now[3 * h + 2]
        return terms[4]
    lax.fori_loop(0, N // 4, force_body, force_terms(0))

    for c in range(3):
        pack(S_R + c, r.at[c])
        send_faces(S_R + c, r.at[c])
    send_faces(S_W, w, n=3)

    def mass_terms(i):
        ay = [rho_f[h, i, ROWS, :] + rho_f[h, i, BELOW, :] for h in range(2)]
        aym = z_below(ay[0], ay[1], to_first(zrho, i))
        return ay[0] + aym[0], ay[1] + aym[1]

    def mass_body(i, before):
        terms = [before] + [mass_terms(4 * i + j + 1) for j in range(4)]
        for j in range(4):
            for h in range(2):
                mass[h, 4 * i + j] = 0.125 * (terms[j][h] + terms[j + 1][h]) + 1.2
        return terms[4]
    lax.fori_loop(0, N // 4, mass_body, mass_terms(0))

    zero_tile = jnp.zeros((8, LANES), F32)

    def receive(slot, field):
        wait_faces(slot, field)
        unpack_rows(slot, field)
        return z_halos(slot)

    for c in range(3):
        ends = receive(S_R + c, r.at[c])

        def image_body(xs, carry, c=c, ends=ends):
            m0, m1, m2 = carry
            pack_planes(S_Q + c, q.at[c], lagging(xs))
            for x, centre, near in neighbours(r.at[c], xs, ends):
                for h in range(2):
                    image = mass[h, x] * centre[h] + 0.2 * near[h]
                    q[c, h, x + 1, ROWS, :] = image
                    nr[c, h, x] = near[h]
                    m0 = m0 + fold(centre[h] * centre[h])
                    m1 = m1 + fold(centre[h] * image)
                    m2 = m2 + fold(image * image)
                    pack_rows(S_Q + c, h, x, image)
            return m0, m1, m2
        moments = planes(image_body, (zero_tile, zero_tile, zero_tile))
        pack_last(S_Q + c, q.at[c])
        send_faces(S_Q + c, q.at[c])
        for k, m in enumerate(moments):
            mom[4 * c + k:4 * c + k + 1, :] = jnp.sum(m, axis=0, keepdims=True)

    def near_w(c):
        unpack_rows(S_W + c, w.at[c])
        ends = z_halos(S_W + c)

        def body(xs, carry):
            for x, _centre, near in neighbours(w.at[c], xs, ends):
                for h in range(2):
                    nw[c, h, x] = near[h]
            return carry
        planes(body)

    for c in range(3):
        ends = receive(S_Q + c, q.at[c])

        def second_body(xs, m3, c=c, ends=ends):
            for x, centre, near in neighbours(q.at[c], xs, ends):
                for h in range(2):
                    nq[c, h, x] = near[h]
                    m3 = m3 + fold(centre[h] * (mass[h, x] * centre[h] + 0.2 * near[h]))
            return m3
        m3 = planes(second_body, zero_tile)
        mom[4 * c + 3:4 * c + 4, :] = jnp.sum(m3, axis=0, keepdims=True)
    mom[12:16, :] = jnp.zeros((4, LANES), F32)

    total = jnp.sum(mom[...], axis=1, keepdims=True)
    on_row = lax.broadcasted_iota(jnp.int32, (16, LANES), 0)
    on_lane = lax.broadcasted_iota(jnp.int32, (16, LANES), 1)
    ar1[0] = jnp.sum(jnp.where(on_row == on_lane, total, 0.0), axis=0, keepdims=True)

    def reduce_copies(buf, send, recv, peer, peers):
        return [
            pltpu.make_async_remote_copy(
                src_ref=buf.at[0], dst_ref=buf.at[k], send_sem=send.at[k], recv_sem=recv.at[k],
                device_id=peer(k), device_id_type=MESH)
            for k in range(1, peers)
        ]

    def gathered(buf, copies):
        for copy in copies:
            copy.wait_recv()
        parts = [buf[k] for k in range(len(copies) + 1)]
        while len(parts) > 1:
            parts = [a + b for a, b in zip(parts[::2], parts[1::2])]
        return parts[0]

    along = reduce_copies(ar1, a1s, a1r, z_peer, nz)
    for copy in along:
        copy.start()
    def mask_body(x, _):
        for h in range(2):
            free[h, x] = 0.8 - 0.8 * pin[h, x].astype(F32)
        return 0
    lax.fori_loop(0, N, mask_body, 0)
    wait_faces(S_W, w, n=3)
    drain(S_P, S_RHO, S_W, *range(S_R, S_R + 3), *range(S_Q, S_Q + 3))
    near_w(0)
    ar2[0] = gathered(ar1, along)
    across = reduce_copies(ar2, a2s, a2r, xy_peer, nxy)
    for copy in across:
        copy.start()
    near_w(1)
    near_w(2)
    sums = gathered(ar2, across)
    row_lane = lax.broadcasted_iota(jnp.int32, (1, LANES), 1)

    def pick(k):
        return jnp.sum(jnp.where(row_lane == k, sums, 0.0), axis=1, keepdims=True)

    for c in range(3):
        m0, m1, m2, m3 = [pick(4 * c + k) for k in range(4)]
        a1 = m0 / m1
        new = m0 - 2.0 * a1 * m1 + a1 * a1 * m2
        b1 = 1.0 + new / m0
        a2 = new / (b1 * b1 * m1 - 2.0 * a1 * b1 * m2 + a1 * a1 * m3)
        c1 = jnp.broadcast_to(a1 + a2 * b1, (N, LANES))
        c2 = jnp.broadcast_to(-a1 * a2, (N, LANES))

        def step_body(xs, carry, c=c, c1=c1, c2=c2):
            pack_planes(S_ONE + c, one.at[c], lagging(xs))
            for x in xs:
                i = x + 1
                for h in range(2):
                    a = c1 * r[c, h, i, ROWS, :] + c2 * q[c, h, i, ROWS, :]
                    acc[c, h, x] = a
                    v = vel[c, h, i, ROWS, :] + 0.6 * a
                    vel[c, h, i, ROWS, :] = v
                    moved = w[c, h, i, ROWS, :] + 0.36 * a
                    w[c, h, i, ROWS, :] = moved
                    near = nw[c, h, x] + 0.36 * (c1 * nr[c, h, x] + c2 * nq[c, h, x])
                    u = moved + free[h, x] * (near * (1.0 / 6.0) - moved)
                    one[c, h, i, ROWS, :] = u
                    pack_rows(S_ONE + c, h, x, u)
            return carry
        planes(step_body)
        pack_last(S_ONE + c, one.at[c])
        send_faces(S_ONE + c, one.at[c])
    for c in range(3):
        pack(S_VEL + c, vel.at[c], (0,))
    send_faces(S_VEL, vel, (0, 2, 4), 3)
    send_edges(S_VEL, E_VEL, -1, 3)

    two = r

    def swept(field, c, xs, ends):
        return [
            (x, [centre[h] + free[h, x] * (near[h] * (1.0 / 6.0) - centre[h]) for h in range(2)])
            for x, centre, near in neighbours(field.at[c], xs, ends)
        ]

    for c in range(3):
        ends = receive(S_ONE + c, one.at[c])

        def sweep_body(xs, carry, c=c, ends=ends):
            pack_planes(S_TWO + c, two.at[c], lagging(xs))
            for x, u in swept(one, c, xs, ends):
                for h in range(2):
                    two[c, h, x + 1, ROWS, :] = u[h]
                    pack_rows(S_TWO + c, h, x, u[h])
            return carry
        planes(sweep_body)
        pack_last(S_TWO + c, two.at[c])
        send_faces(S_TWO + c, two.at[c])

    wait_faces(S_VEL, vel, (0, 2, 4), 3)
    wait_edges(S_VEL, E_VEL, -1, 3)
    for c in range(3):
        edge_halo(S_VEL + c, E_VEL + c, vel.at[c], -1)

    def rows_up(k):
        return ze[k, ROWS, :], ze[k, ABOVE, :]

    zx, zy, zz3 = rows_up(E_VEL), rows_up(E_VEL + 1), rows_up(E_VEL + 2)
    z_s1 = (zy[1] - zy[0]) + (zz3[0] + zz3[1])
    z_s2 = zx[0] + zx[1]

    def div_terms(i):
        s1, s2, s3 = [], [], []
        for h in range(2):
            ax = vel[0, h, i, ROWS, :] + vel[0, h, i, ABOVE, :]
            dy = vel[1, h, i, ABOVE, :] - vel[1, h, i, ROWS, :]
            az = vel[2, h, i, ROWS, :] + vel[2, h, i, ABOVE, :]
            s1.append(dy + az)
            s2.append(ax)
            s3.append(dy - az)
        u1 = z_above(s1[0], s1[1], to_last(z_s1, i))
        u2 = z_above(s2[0], s2[1], to_last(z_s2, i))
        plus, minus = [], []
        for h in range(2):
            flat, along_x = s3[h] + u1[h], s2[h] + u2[h]
            plus.append(flat + along_x)
            minus.append(flat - along_x)
        return plus, minus

    def div_body(k, before):
        back = jnp.maximum(2 * k - 2, 0)
        pack_planes(S_DE, de, [back, back + 1])
        for j in range(2):
            x = 2 * k + j
            plus, minus = div_terms(x + 2)
            for h in range(2):
                spread = before[h] + plus[h]
                value = rho_f[h, x + 1, ROWS, :] * (en[h, x] * (1.0 - 0.06 * spread))
                de[h, x + 1, ROWS, :] = value
                pack_rows(S_DE, h, x, value)
            before = minus
        return tuple(before)
    lax.fori_loop(0, N // 2, div_body, tuple(div_terms(1)[1]))
    pack_last(S_DE, de, 2)
    send_faces(S_DE, de)

    for c in range(3):
        ends = receive(S_TWO + c, two.at[c])

        def last_body(xs, carry, c=c, ends=ends):
            pack_planes(S_SH + c, sh.at[c], lagging(xs))
            for x, u in swept(two, c, xs, ends):
                for h in range(2):
                    relaxed[c, h, x] = u[h]
                    s = u[h] - w[c, h, x + 1, ROWS, :]
                    sh[c, h, x + 1, ROWS, :] = s
                    pack_rows(S_SH + c, h, x, s, (0,))
            return carry
        planes(last_body)
        pack_last(S_SH + c, sh.at[c])
        send_faces(S_SH + c, sh.at[c], (4, 2, 0))
        send_edges(S_SH + c, E_SH + c, -1)

    drain(*range(S_ONE, S_ONE + 3), *range(S_TWO, S_TWO + 3), S_VEL, S_DE)
    receive(S_DE, de)
    fields = (rho_f, de)
    wide = pl.ds(8, 40)
    wide_last = lax.broadcasted_iota(jnp.int32, (40, LANES), 1) == LANES - 1

    def receive_shift(c):
        wait_faces(S_SH + c, sh.at[c], (4, 2, 0))
        wait_edges(S_SH + c, E_SH + c, -1)
        edge_halo(S_SH + c, E_SH + c, sh.at[c], -1)
        return rows_up(E_SH + c)

    zx = receive_shift(0)
    z_ax = zx[0] + zx[1]

    def flux_x(i):
        a = [sh[0, h, i, ROWS, :] + sh[0, h, i, ABOVE, :] for h in range(2)]
        up = z_above(a[0], a[1], to_last(z_ax, i))
        out = []
        for h in range(2):
            s = 0.25 * (a[h] + up[h])
            for field in fields:
                out.append(s * jnp.where(s > 0, field[h, i, ROWS, :], field[h, i - 1, ROWS, :]))
        return tuple(out)

    def remap_x(k, before):
        for j in range(2):
            x = 2 * k + j
            now = flux_x(x + 2)
            for h in range(2):
                for f, field in enumerate(fields):
                    partial[f, h, x] = field[h, x + 1, ROWS, :] + (now[2 * h + f] - before[2 * h + f])
            before = now
        return before
    lax.fori_loop(0, N // 2, remap_x, flux_x(1))

    receive_shift(1)
    z_y = ze[E_SH + 1, wide, :]
    z_y = z_y + pltpu.roll(z_y, LANES - 2, 1)

    def remap_y(xs, carry):
        for j, x in enumerate(xs):
            i = x + 1
            t = [sh[1, h, i, wide, :] + sh[1, h, i + 1, wide, :] for h in range(2)]
            ra, rb = [pltpu.roll(v, LANES - 1, 1) for v in t]
            up = (jnp.where(wide_last, rb, ra), jnp.where(wide_last, to_last(z_y, i), rb))
            for h in range(2):
                s = 0.25 * (t[h] + up[h])
                for f, field in enumerate(fields):
                    gy[j, f, h] = s * jnp.where(s > 0, field[h, i, wide, :], field[h, i, pl.ds(7, 40), :])
        for j, x in enumerate(xs):
            for h in range(2):
                for f in range(2):
                    partial[f, h, x] = partial[f, h, x] + (gy[j, f, h, 1:N + 1, :] - gy[j, f, h, 0:N, :])
        return carry
    planes(remap_y, 0, 2)

    zz3 = receive_shift(2)
    z_z = zz3[0] + zz3[1]
    z_z = 0.25 * (z_z + pltpu.roll(z_z, LANES - 2, 1))
    for f, slot in enumerate((S_RHO, S_DE)):
        tab[f] = jnp.where(
            odd, z_halo(slot, 0), z_z * jnp.where(z_z > 0, z_halo(slot, 1), zs[slot]))

    for copy in along + across:
        copy.wait_send()
    drain(*sent)


def remap(
    vel, acc, relaxed, sh, de, rho_f, tab, partial,
    v_out, a_out, r_out, d_out, e_out,
    nr, out_sem,
):
    fields = (rho_f, de)
    outs = []

    def halves(k):
        return pl.ds(k * LANES, LANES)

    def write(src, dst, i, h):
        copy = pltpu.make_async_copy(src, dst, out_sem.at[i, h])
        copy.start()
        outs.append(copy)

    for c in range(3):
        for h in range(2):
            write(acc.at[c, h], a_out.at[c, :, :, halves(h)], c, h)
            write(vel.at[c, h, pl.ds(1, N), ROWS, :], v_out.at[c, :, :, halves(h)], 3 + c, h)
            write(relaxed.at[c, h], r_out.at[c, :, :, halves(h)], 6 + c, h)
    def remap_z(xs, carry):
        for x in xs:
            i = x + 1
            s = [
                0.25 * ((sh[2, h, i, ROWS, :] + sh[2, h, i, ABOVE, :])
                        + (sh[2, h, i + 1, ROWS, :] + sh[2, h, i + 1, ABOVE, :]))
                for h in range(2)
            ]
            for f, field in enumerate(fields):
                own = [field[h, i, ROWS, :] for h in range(2)]
                end = to_ends(tab[f], i)
                under = z_below(own[0], own[1], end)
                g = [s[h] * jnp.where(s[h] > 0, own[h], under[h]) for h in range(2)]
                over = z_above(g[0], g[1], end)
                for h in range(2):
                    nr[f, h, x] = partial[f, h, x] + (over[h] - g[h])
        return carry
    for part in range(4):
        lo = 8 * part
        planes(remap_z, 0, 2, lo, lo + 8)
        for f, out in enumerate((d_out, e_out)):
            for h in range(2):
                write(nr.at[f, h, pl.ds(lo, 8)], out.at[pl.ds(lo, 8), :, halves(h)], 9 + 4 * f + part, h)
    for copy in outs:
        copy.wait()


def solution(mesh):
    sizes = tuple(mesh.shape[name] for name in ("bx", "by", "bz"))
    vector = P(None, "bx", "by", "bz")
    scalar = P("bx", "by", "bz")

    def on_device(position, velocity, density, energy, pinned):
        def padded(*lead):
            return pltpu.VMEM(lead + (2, PX, PY, LANES), F32)

        def plain(*lead, dtype=F32):
            return pltpu.VMEM(lead + (2, N, N, LANES), dtype)

        dma = pltpu.SemaphoreType.DMA
        v3 = jax.ShapeDtypeStruct(position.shape, F32)
        v1 = jax.ShapeDtypeStruct(density.shape, F32)
        anywhere = pl.BlockSpec(memory_space=pl.ANY)

        def body(*refs):
            kernel(sizes, *refs)

        in_vmem = pl.BlockSpec(memory_space=pltpu.VMEM)
        handed = pl.pallas_call(
            body,
            name="lagrangian_step",
            out_shape=(
                padded(3), plain(3), plain(3), padded(3), padded(), padded(), pltpu.VMEM((2, N, LANES), F32),
                plain(2)),
            in_specs=[anywhere] * 5,
            out_specs=[in_vmem] * 8,
            scratch_shapes=[
                padded(), plain(), padded(3), padded(3), padded(3),
                plain(3), plain(3), plain(3), plain(dtype=jnp.int32), plain(), plain(),
                padded(3),
                pltpu.VMEM((SLOTS, 2, 2, N, 1, LANES), F32),
                pltpu.VMEM((SLOTS, 2, 2, N, 1, LANES), F32),
                pltpu.VMEM((SLOTS, N, LANES), F32),
                pltpu.VMEM((SLOTS, 2, N, LANES), F32),
                pltpu.VMEM((EDGES, 2, 1, LANES), F32),
                pltpu.VMEM((EDGES, N, LANES), F32),
                pltpu.VMEM((EDGES, 8, LANES), F32),
                pltpu.VMEM((EDGES, 8, LANES), F32),
                pltpu.VMEM((EDGES, PY, LANES), F32),
                pltpu.VMEM((2 * LANES, 2 * LANES), jnp.bfloat16),
                pltpu.VMEM((2, 2, 2, 40, LANES), F32),
                pltpu.VMEM((16, LANES), F32),
                pltpu.VMEM((sizes[2], 1, LANES), F32),
                pltpu.VMEM((sizes[0] * sizes[1], 1, LANES), F32),
                dma((5, 2)),
                dma((SLOTS, 6)), dma((SLOTS, 6)), dma((EDGES, 4)), dma((EDGES, 4)),
                dma((sizes[2],)), dma((sizes[2],)),
                dma((sizes[0] * sizes[1],)), dma((sizes[0] * sizes[1],)),
            ],
            compiler_params=pltpu.CompilerParams(
                collective_id=0, has_side_effects=True, vmem_limit_bytes=42 * 1000 * 1000),
        )(position, velocity, density, energy, pinned)
        return tuple(pl.pallas_call(
            remap,
            name="remap",
            out_shape=(v3, v3, v3, v1, v1),
            in_specs=[in_vmem] * 8,
            out_specs=[anywhere] * 5,
            scratch_shapes=[plain(2), dma((17, 2))],
            compiler_params=pltpu.CompilerParams(vmem_limit_bytes=4 * 1000 * 1000),
        )(*handed))

    return jax.shard_map(
        on_device,
        mesh=mesh,
        in_specs=(vector, vector, scalar, scalar, scalar),
        out_specs=(vector, vector, vector, scalar, scalar),
        check_vma=False,
    )
```

```python
import jax
import jax.numpy as jnp
from jax import lax
from jax.experimental import pallas as pl
from jax.experimental.pallas import tpu as pltpu
from jax.sharding import PartitionSpec as P

MESH = pl.DeviceIdType.MESH
F32 = jnp.float32
N = 32
LANES = 128
PX = N + 2
PY = 48
TRIP = 16
ROWS = pl.ds(8, N)
BELOW = pl.ds(7, N)
ABOVE = pl.ds(9, N)

S_P, S_RHO, S_W, S_R, S_Q, S_ONE, S_TWO, S_VEL, S_SH, S_DE = 0, 1, 2, 5, 8, 11, 14, 17, 20, 23
SLOTS = 24
E_P, E_RHO, E_VEL, E_SH = 0, 1, 2, 5
EDGES = 8


def _lane():
    return lax.broadcasted_iota(jnp.int32, (N, LANES), 1)


def planes(body, init=0, trip=TRIP, start=0, stop=N):
    def run(i, carry):
        return body([i * trip + j for j in range(trip)], carry)
    return lax.fori_loop(start // trip, stop // trip, run, init)


def z_below(a, b, halo):
    ra, rb = pltpu.roll(a, 1, 1), pltpu.roll(b, 1, 1)
    return jnp.where(_lane() == 0, halo, ra), jnp.where(_lane() == 0, ra, rb)


def z_above(a, b, halo):
    ra, rb = pltpu.roll(a, LANES - 1, 1), pltpu.roll(b, LANES - 1, 1)
    return jnp.where(_lane() == LANES - 1, rb, ra), jnp.where(_lane() == LANES - 1, halo, rb)


def to_ends(z, i):
    return pltpu.roll(z, LANES - 1 - 2 * i, 1)


def to_last(z, i):
    return pltpu.roll(z, LANES - 1 - 2 * i, 1)


def to_first(z, i):
    return pltpu.roll(z, LANES - 1 - 2 * i, 1)


def kernel(
    sizes,
    pos_in, vel_in, rho_in, en_in, pin_in,
    vel, acc, relaxed, sh, de, rho_f, tab, partial,
    pres, en, w, r, q, nw, nr, nq, pin, free, mass, one,
    ys, yr, zs, zr, exy, exz, eyz, exyz, ze, band, gy, mom, ar1, ar2,
    in_sem, face_s, face_r, edge_s, edge_r, a1s, a1r, a2s, a2r,
):
    names = ("bx", "by", "bz")
    here = [lax.axis_index(name) for name in names]

    def exists(step):
        ok = None
        for i in range(3):
            if step[i] == 0:
                continue
            one_ok = here[i] + step[i] >= 0 if step[i] < 0 else here[i] + step[i] < sizes[i]
            ok = one_ok if ok is None else jnp.logical_and(ok, one_ok)
        return ok

    def device(step):
        return tuple(lax.rem(here[i] + step[i] + sizes[i], sizes[i]) for i in range(3))

    def flag(step):
        return exists(step).astype(jnp.int32) > 0

    def neg(step):
        return tuple(-s for s in step)

    steps = ((-1, 0, 0), (1, 0, 0), (0, -1, 0), (0, 1, 0), (0, 0, -1), (0, 0, 1))
    lane = lax.broadcasted_iota(jnp.int32, (N, LANES), 1)

    def some(slot, n):
        return slot if n == 1 else pl.ds(slot, n)

    def face_copy(slot, field, d, n=1):
        at = some(slot, n)
        if d < 2:
            src, dst = ((1, PX - 1), (N, 0))[d]
            lead = () if n == 1 else (slice(None),)
            src, dst = [field.at[lead + (slice(None), plane, ROWS, slice(None))] for plane in (src, dst)]
        elif d < 4:
            src, dst = ys.at[at, d - 2], yr.at[at, 3 - d]
        else:
            src, dst = zs.at[at], zr.at[at, 5 - d]
        return pltpu.make_async_remote_copy(
            src_ref=src, dst_ref=dst, send_sem=face_s.at[slot, d], recv_sem=face_r.at[slot, d],
            device_id=device(steps[d]), device_id_type=MESH)

    def edge_copies(slot, eslot, sign, n=1):
        at, to = some(slot, n), some(eslot, n)
        side = 1 if sign > 0 else 0
        row = N - 1 if sign > 0 else 0
        tile = pl.ds(N - 8, 8) if sign > 0 else pl.ds(0, 8)
        pieces = (
            ((sign, sign, 0), ys.at[at, side, :, row], exy.at[to]),
            ((sign, 0, sign), zs.at[at], exz.at[to]),
            ((0, sign, sign), zs.at[at, tile], eyz.at[to]),
            ((sign, sign, sign), zs.at[at, tile], exyz.at[to]),
        )
        return [
            (step, pltpu.make_async_remote_copy(
                src_ref=src, dst_ref=dst, send_sem=edge_s.at[eslot, i], recv_sem=edge_r.at[eslot, i],
                device_id=device(step), device_id_type=MESH))
            for i, (step, src, dst) in enumerate(pieces)
        ]

    sent = {}

    def drain(*slots):
        for slot in slots:
            for step, copy in sent.pop(slot, ()):
                pl.when(exists(step))(copy.wait_send)

    def send_faces(slot, field, ds=(0, 1, 2, 3, 4, 5), n=1):
        for d in ds:
            copy = face_copy(slot, field, d, n)
            pl.when(exists(steps[d]))(copy.start)
            sent.setdefault(slot, []).append((steps[d], copy))

    def send_edges(slot, eslot, sign, n=1):
        for step, copy in edge_copies(slot, eslot, sign, n):
            pl.when(exists(step))(copy.start)
            sent.setdefault(slot, []).append((step, copy))

    def wait_faces(slot, field, ds=(0, 1, 2, 3, 4, 5), n=1):
        for d in ds:
            pl.when(exists(neg(steps[d])))(face_copy(slot, field, d, n).wait_recv)

    def wait_edges(slot, eslot, sign, n=1):
        for step, copy in edge_copies(slot, eslot, sign, n):
            pl.when(exists(neg(step)))(copy.wait_recv)

    zero_plane = jnp.zeros((N, LANES), F32)
    odd = lane % 2 == 1
    left = lane < LANES // 2

    def lagging(xs):
        back = jnp.minimum(xs[0], len(xs))
        return [x - back for x in xs]

    def pack_planes(slot, field, xs):
        mixed = [
            pltpu.roll(jnp.where(left, field[0, x + 1, ROWS, :], field[1, x + 1, ROWS, :]), 2 * x + 3, 1)
            for x in xs
        ]
        z = zs[slot]
        for x, m in zip(xs, mixed):
            z = jnp.where((lane >> 1) == x + 1, m, z)
        zs[slot] = z

    def pack_last(slot, field, trip=TRIP):
        pack_planes(slot, field, list(range(N - trip, N)))

    def pack_rows(slot, h, x, v, sides=(0, 1)):
        if 0 in sides:
            ys[slot, 0, h, x] = v[0:1]
        if 1 in sides:
            ys[slot, 1, h, x] = v[N - 1:N]

    def pack(slot, field, sides=(0, 1)):
        def body(xs, carry):
            pack_planes(slot, field, xs)
            for x in xs:
                for h in range(2):
                    for s in sides:
                        row = 8 if s == 0 else 7 + N
                        ys[slot, s, h, x] = field[h, x + 1, row:row + 1, :]
            return carry
        planes(body, 0, 16)

    def unpack_rows(slot, field, sides=(0, 1)):
        have = [flag((0, -1, 0)), flag((0, 1, 0))]

        def body(x, _):
            for s in sides:
                row = 7 if s == 0 else 8 + N
                for h in range(2):
                    got = yr[slot, s, h, x]
                    field[h, x + 1, row:row + 1, :] = jnp.where(have[s], got, jnp.zeros_like(got))
            return 0
        lax.fori_loop(0, N, body, 0, unroll=4)

    def z_halo(slot, side):
        have = flag((0, 0, -1 if side == 0 else 1))
        return jnp.where(have, pltpu.roll(zr[slot, side], 1 if side == 0 else LANES - 1, 1), zero_plane)

    def z_halos(slot):
        return jnp.where(odd, z_halo(slot, 0), z_halo(slot, 1))

    def edge_halo(slot, eslot, field, sign):
        side = 0 if sign > 0 else 1
        unpack_rows(slot, field, (side,))
        step = -sign
        plane, row = (0, 7) if sign > 0 else (PX - 1, 8 + N)
        have = flag((step, step, 0))
        for h in range(2):
            got = exy[eslot, h]
            field[h, plane, row:row + 1, :] = jnp.where(have, got, jnp.zeros_like(got))
        turn, at = (LANES // 2 + 1, 1) if sign > 0 else (2 * N - 1, 2 * N + 2)
        whole = 1 if sign > 0 else LANES - 1
        beside = jnp.where(flag((step, 0, step)), exz[eslot], zero_plane)
        ze[eslot, ROWS, :] = jnp.where(lane == at, pltpu.roll(beside, turn, 1), z_halo(slot, side))
        tile_lane = lax.broadcasted_iota(jnp.int32, (8, LANES), 1)
        zero_tile = jnp.zeros((8, LANES), F32)
        corner = jnp.where(flag((step, step, step)), exyz[eslot], zero_tile)
        across = jnp.where(flag((0, step, step)), eyz[eslot], zero_tile)
        tile = pl.ds(0, 8) if sign > 0 else pl.ds(8 + N, 8)
        ze[eslot, tile, :] = jnp.where(
            tile_lane == at, pltpu.roll(corner, turn, 1), pltpu.roll(across, whole, 1))

    def clear_missing(field, planes=(0, PX - 1)):
        for plane in planes:
            step = (-1, 0, 0) if plane == 0 else (1, 0, 0)

            @pl.when(jnp.logical_not(exists(step)))
            def _():
                for h in range(2):
                    field[h, plane, ROWS, :] = zero_plane

    at_row = lax.broadcasted_iota(jnp.int32, (2 * LANES, 2 * LANES), 0)
    at_column = lax.broadcasted_iota(jnp.int32, (2 * LANES, 2 * LANES), 1)
    band[...] = jnp.where(jnp.abs(at_row - at_column) == 1, 1.0, 0.0).astype(jnp.bfloat16)

    def neighbours(field, xs, ends):
        both = [
            jnp.concatenate([field[h, x + 1, ROWS, :] for x in xs], axis=0) for h in range(2)
        ]
        whole = jnp.concatenate(both, axis=1)
        lead = whole.astype(jnp.bfloat16)
        rest = (whole - lead.astype(F32)).astype(jnp.bfloat16)
        along_z = jnp.dot(lead, band[...], preferred_element_type=F32) + jnp.dot(
            rest, band[...], preferred_element_type=F32)
        out = []
        for j, x in enumerate(xs):
            i = x + 1
            end = to_ends(ends, i)
            edge = (jnp.where(lane == 0, end, 0.0), jnp.where(lane == LANES - 1, end, 0.0))
            centre = [field[h, i, ROWS, :] for h in range(2)]
            near = []
            for h in range(2):
                s = (field[h, i - 1, ROWS, :] + field[h, i + 1, ROWS, :]) + (
                    field[h, i, BELOW, :] + field[h, i, ABOVE, :])
                z = along_z[N * j:N * j + N, LANES * h:LANES * h + LANES]
                near.append(s + (z + edge[h]))
            out.append((x, centre, near))
        return out

    def fold(v):
        return (v[0:8] + v[8:16]) + (v[16:24] + v[24:32])

    def halves(k):
        return pl.ds(k * LANES, LANES)

    loads = {}
    for h in range(2):
        loads["rho", h] = pltpu.make_async_copy(
            rho_in.at[:, :, halves(h)], rho_f.at[h, pl.ds(1, N), ROWS, :], in_sem.at[0, h])
        loads["en", h] = pltpu.make_async_copy(en_in.at[:, :, halves(h)], en.at[h], in_sem.at[1, h])
        loads["vel", h] = pltpu.make_async_copy(
            vel_in.at[:, :, :, halves(h)], vel.at[:, h, pl.ds(1, N), ROWS, :], in_sem.at[2, h])
        loads["pos", h] = pltpu.make_async_copy(
            pos_in.at[:, :, :, halves(h)], w.at[:, h, pl.ds(1, N), ROWS, :], in_sem.at[3, h])
        loads["pin", h] = pltpu.make_async_copy(pin_in.at[:, :, halves(h)], pin.at[h], in_sem.at[4, h])
    for name in ("rho", "en", "vel", "pos", "pin"):
        for h in range(2):
            loads[name, h].start()

    clear_missing(pres, (0,))
    clear_missing(rho_f)
    clear_missing(de)
    for c in range(3):
        for field in (w, r, q, one):
            clear_missing(field.at[c])
        for field in (vel, sh):
            clear_missing(field.at[c], (PX - 1,))

    barrier = pltpu.get_barrier_semaphore()
    around = [s for s in ((i, j, k) for i in (0, 1) for j in (0, 1) for k in (0, 1)) if any(s)]
    around = around + [neg(s) for s in around]
    count = 0
    for step in around:
        @pl.when(exists(step))
        def _():
            pl.semaphore_signal(barrier, inc=1, device_id=device(step), device_id_type=MESH)
        count = count + exists(step).astype(jnp.int32)
    nz, nxy = sizes[2], sizes[0] * sizes[1]

    def z_peer(k):
        return (here[0], here[1], lax.rem(here[2] + k, nz))

    def xy_peer(k):
        return (lax.rem(here[0] + k // sizes[1], sizes[0]), lax.rem(here[1] + k % sizes[1], sizes[1]), here[2])

    for k in range(1, nz):
        pl.semaphore_signal(barrier, inc=1, device_id=z_peer(k), device_id_type=MESH)
    for k in range(1, nxy):
        pl.semaphore_signal(barrier, inc=1, device_id=xy_peer(k), device_id_type=MESH)

    for name in ("rho", "en"):
        for h in range(2):
            loads[name, h].wait()

    def pressure_body(xs, carry):
        back = lagging(xs)
        pack_planes(S_P, pres, back)
        pack_planes(S_RHO, rho_f, xs)
        for x in xs:
            for h in range(2):
                rho = rho_f[h, x + 1, ROWS, :]
                p = 0.1 * rho * en[h, x]
                pres[h, x + 1, ROWS, :] = p
                pack_rows(S_P, h, x, p, (1,))
                pack_rows(S_RHO, h, x, rho)
        return carry

    planes(pressure_body)
    pack_last(S_P, pres)

    pl.semaphore_wait(barrier, count + (nz - 1) + (nxy - 1))
    send_edges(S_P, E_P, 1, 2)
    send_faces(S_P, None, (5, 3), 2)
    send_faces(S_P, pres, (1,))
    send_faces(S_RHO, rho_f, (1, 4, 2, 0))

    for name in ("vel", "pos", "pin"):
        for h in range(2):
            loads[name, h].wait()

    def advance(c):
        def body(xs, carry):
            pack_planes(S_W + c, w.at[c], lagging(xs))
            for x in xs:
                for h in range(2):
                    v = w[c, h, x + 1, ROWS, :] + 0.6 * vel[c, h, x + 1, ROWS, :]
                    w[c, h, x + 1, ROWS, :] = v
                    pack_rows(S_W + c, h, x, v)
            return carry
        planes(body)
        pack_last(S_W + c, w.at[c])
        if c < 2:
            send_faces(S_W + c, w.at[c])

    for c in range(3):
        advance(c)

    wait_faces(S_P, None, (5, 3), 2)
    wait_edges(S_P, E_P, 1, 2)
    wait_faces(S_P, pres, (1,))
    wait_faces(S_RHO, rho_f, (1, 4, 2, 0))
    edge_halo(S_P, E_P, pres, 1)
    edge_halo(S_RHO, E_RHO, rho_f, 1)
    unpack_rows(S_RHO, rho_f, (1,))
    zay = ze[E_P, ROWS, :] + ze[E_P, BELOW, :]
    zdy = ze[E_P, BELOW, :] - ze[E_P, ROWS, :]
    zrho = ze[E_RHO, ROWS, :] + ze[E_RHO, BELOW, :]

    def force_terms(i):
        ay, dy = [], []
        for h in range(2):
            c, b = pres[h, i, ROWS, :], pres[h, i, BELOW, :]
            ay.append(c + b)
            dy.append(b - c)
        aym = z_below(ay[0], ay[1], to_first(zay, i))
        dym = z_below(dy[0], dy[1], to_first(zdy, i))
        return tuple(
            t for h in range(2) for t in (ay[h] + aym[h], dy[h] + dym[h], aym[h] - ay[h]))

    def force_body(i, before):
        terms = [before] + [force_terms(4 * i + j + 1) for j in range(4)]
        for j in range(4):
            old, now = terms[j], terms[j + 1]
            for h in range(2):
                r[0, h, 4 * i + j + 1, ROWS, :] = old[3 * h] - now[3 * h]
                r[1, h, 4 * i + j + 1, ROWS, :] = old[3 * h + 1] + now[3 * h + 1]
                r[2, h, 4 * i + j + 1, ROWS, :] = old[3 * h + 2] + now[3 * h + 2]
        return terms[4]
    lax.fori_loop(0, N // 4, force_body, force_terms(0))

    for c in range(3):
        pack(S_R + c, r.at[c])
        send_faces(S_R + c, r.at[c])
    send_faces(S_W + 2, w.at[2])

    def mass_terms(i):
        ay = [rho_f[h, i, ROWS, :] + rho_f[h, i, BELOW, :] for h in range(2)]
        aym = z_below(ay[0], ay[1], to_first(zrho, i))
        return ay[0] + aym[0], ay[1] + aym[1]

    def mass_body(i, before):
        terms = [before] + [mass_terms(4 * i + j + 1) for j in range(4)]
        for j in range(4):
            for h in range(2):
                mass[h, 4 * i + j] = 0.125 * (terms[j][h] + terms[j + 1][h]) + 1.2
        return terms[4]
    lax.fori_loop(0, N // 4, mass_body, mass_terms(0))

    zero_tile = jnp.zeros((8, LANES), F32)

    def receive(slot, field):
        wait_faces(slot, field)
        unpack_rows(slot, field)
        return z_halos(slot)

    def near_w(c):
        ends = receive(S_W + c, w.at[c])

        def body(xs, carry):
            for x, _centre, near in neighbours(w.at[c], xs, ends):
                for h in range(2):
                    nw[c, h, x] = near[h]
            return carry
        planes(body)

    near_w(0)
    for c in range(3):
        ends = receive(S_R + c, r.at[c])

        def image_body(xs, carry, c=c, ends=ends):
            m0, m1, m2 = carry
            pack_planes(S_Q + c, q.at[c], lagging(xs))
            for x, centre, near in neighbours(r.at[c], xs, ends):
                for h in range(2):
                    image = mass[h, x] * centre[h] + 0.2 * near[h]
                    q[c, h, x + 1, ROWS, :] = image
                    nr[c, h, x] = near[h]
                    m0 = m0 + fold(centre[h] * centre[h])
                    m1 = m1 + fold(centre[h] * image)
                    m2 = m2 + fold(image * image)
                    pack_rows(S_Q + c, h, x, image)
            return m0, m1, m2
        moments = planes(image_body, (zero_tile, zero_tile, zero_tile))
        pack_last(S_Q + c, q.at[c])
        send_faces(S_Q + c, q.at[c])
        for k, m in enumerate(moments):
            mom[4 * c + k:4 * c + k + 1, :] = jnp.sum(m, axis=0, keepdims=True)

    for c in range(3):
        ends = receive(S_Q + c, q.at[c])

        def second_body(xs, m3, c=c, ends=ends):
            for x, centre, near in neighbours(q.at[c], xs, ends):
                for h in range(2):
                    nq[c, h, x] = near[h]
                    m3 = m3 + fold(centre[h] * (mass[h, x] * centre[h] + 0.2 * near[h]))
            return m3
        m3 = planes(second_body, zero_tile)
        mom[4 * c + 3:4 * c + 4, :] = jnp.sum(m3, axis=0, keepdims=True)
    mom[12:16, :] = jnp.zeros((4, LANES), F32)

    total = jnp.sum(mom[0:16, :], axis=1, keepdims=True)
    on_row = lax.broadcasted_iota(jnp.int32, (16, LANES), 0)
    on_lane = lax.broadcasted_iota(jnp.int32, (16, LANES), 1)
    ar1[0] = jnp.sum(jnp.where(on_row == on_lane, total, 0.0), axis=0, keepdims=True)

    def reduce_copies(buf, send, recv, peer, peers):
        return [
            pltpu.make_async_remote_copy(
                src_ref=buf.at[0], dst_ref=buf.at[k], send_sem=send.at[k], recv_sem=recv.at[k],
                device_id=peer(k), device_id_type=MESH)
            for k in range(1, peers)
        ]

    def gathered(buf, copies):
        for copy in copies:
            copy.wait_recv()
        parts = [buf[k] for k in range(len(copies) + 1)]
        while len(parts) > 1:
            parts = [a + b for a, b in zip(parts[::2], parts[1::2])]
        return parts[0]

    along = reduce_copies(ar1, a1s, a1r, z_peer, nz)
    for copy in along:
        copy.start()
    def mask_body(x, _):
        for h in range(2):
            free[h, x] = 0.8 - 0.8 * pin[h, x].astype(F32)
        return 0
    lax.fori_loop(0, N, mask_body, 0)
    drain(S_P, S_RHO, *range(S_W, S_W + 3), *range(S_R, S_R + 3), *range(S_Q, S_Q + 3))
    near_w(1)
    ar2[0] = gathered(ar1, along)
    across = reduce_copies(ar2, a2s, a2r, xy_peer, nxy)
    for copy in across:
        copy.start()
    near_w(2)
    sums = gathered(ar2, across)
    row_lane = lax.broadcasted_iota(jnp.int32, (1, LANES), 1)

    def pick(k):
        return jnp.sum(jnp.where(row_lane == k, sums, 0.0), axis=1, keepdims=True)

    for c in range(3):
        m0, m1, m2, m3 = [pick(4 * c + k) for k in range(4)]
        a1 = m0 / m1
        new = m0 - 2.0 * a1 * m1 + a1 * a1 * m2
        b1 = 1.0 + new / m0
        a2 = new / (b1 * b1 * m1 - 2.0 * a1 * b1 * m2 + a1 * a1 * m3)
        c1 = jnp.broadcast_to(a1 + a2 * b1, (N, LANES))
        c2 = jnp.broadcast_to(-a1 * a2, (N, LANES))

        def step_body(xs, carry, c=c, c1=c1, c2=c2):
            pack_planes(S_ONE + c, one.at[c], lagging(xs))
            for x in xs:
                i = x + 1
                for h in range(2):
                    a = c1 * r[c, h, i, ROWS, :] + c2 * q[c, h, i, ROWS, :]
                    acc[c, h, x] = a
                    v = vel[c, h, i, ROWS, :] + 0.6 * a
                    vel[c, h, i, ROWS, :] = v
                    moved = w[c, h, i, ROWS, :] + 0.36 * a
                    w[c, h, i, ROWS, :] = moved
                    near = nw[c, h, x] + 0.36 * (c1 * nr[c, h, x] + c2 * nq[c, h, x])
                    u = moved + free[h, x] * (near * (1.0 / 6.0) - moved)
                    one[c, h, i, ROWS, :] = u
                    pack_rows(S_ONE + c, h, x, u)
            return carry
        planes(step_body)
        pack_last(S_ONE + c, one.at[c])
        send_faces(S_ONE + c, one.at[c])
    for c in range(3):
        pack(S_VEL + c, vel.at[c], (0,))
    send_faces(S_VEL, vel, (0, 2, 4), 3)
    send_edges(S_VEL, E_VEL, -1, 3)

    two = r

    def swept(field, c, xs, ends):
        return [
            (x, [centre[h] + free[h, x] * (near[h] * (1.0 / 6.0) - centre[h]) for h in range(2)])
            for x, centre, near in neighbours(field.at[c], xs, ends)
        ]

    for c in range(3):
        ends = receive(S_ONE + c, one.at[c])

        def sweep_body(xs, carry, c=c, ends=ends):
            pack_planes(S_TWO + c, two.at[c], lagging(xs))
            for x, u in swept(one, c, xs, ends):
                for h in range(2):
                    two[c, h, x + 1, ROWS, :] = u[h]
                    pack_rows(S_TWO + c, h, x, u[h])
            return carry
        planes(sweep_body)
        pack_last(S_TWO + c, two.at[c])
        send_faces(S_TWO + c, two.at[c])

    wait_faces(S_VEL, vel, (0, 2, 4), 3)
    wait_edges(S_VEL, E_VEL, -1, 3)
    for c in range(3):
        edge_halo(S_VEL + c, E_VEL + c, vel.at[c], -1)

    def rows_up(k):
        return ze[k, ROWS, :], ze[k, ABOVE, :]

    zx, zy, zz3 = rows_up(E_VEL), rows_up(E_VEL + 1), rows_up(E_VEL + 2)
    z_s1 = (zy[1] - zy[0]) + (zz3[0] + zz3[1])
    z_s2 = zx[0] + zx[1]

    def div_terms(i):
        s1, s2, s3 = [], [], []
        for h in range(2):
            ax = vel[0, h, i, ROWS, :] + vel[0, h, i, ABOVE, :]
            dy = vel[1, h, i, ABOVE, :] - vel[1, h, i, ROWS, :]
            az = vel[2, h, i, ROWS, :] + vel[2, h, i, ABOVE, :]
            s1.append(dy + az)
            s2.append(ax)
            s3.append(dy - az)
        u1 = z_above(s1[0], s1[1], to_last(z_s1, i))
        u2 = z_above(s2[0], s2[1], to_last(z_s2, i))
        plus, minus = [], []
        for h in range(2):
            flat, along_x = s3[h] + u1[h], s2[h] + u2[h]
            plus.append(flat + along_x)
            minus.append(flat - along_x)
        return plus, minus

    def div_body(k, before):
        back = jnp.maximum(4 * k - 4, 0)
        pack_planes(S_DE, de, [back + j for j in range(4)])
        for j in range(4):
            x = 4 * k + j
            plus, minus = div_terms(x + 2)
            for h in range(2):
                spread = before[h] + plus[h]
                value = rho_f[h, x + 1, ROWS, :] * (en[h, x] * (1.0 - 0.06 * spread))
                de[h, x + 1, ROWS, :] = value
                pack_rows(S_DE, h, x, value)
            before = minus
        return tuple(before)
    lax.fori_loop(0, N // 4, div_body, tuple(div_terms(1)[1]))
    pack_last(S_DE, de, 4)
    send_faces(S_DE, de)

    for c in range(3):
        ends = receive(S_TWO + c, two.at[c])

        def last_body(xs, carry, c=c, ends=ends):
            pack_planes(S_SH + c, sh.at[c], lagging(xs))
            for x, u in swept(two, c, xs, ends):
                for h in range(2):
                    relaxed[c, h, x] = u[h]
                    s = u[h] - w[c, h, x + 1, ROWS, :]
                    sh[c, h, x + 1, ROWS, :] = s
                    pack_rows(S_SH + c, h, x, s, (0,))
            return carry
        planes(last_body)
        pack_last(S_SH + c, sh.at[c])
        send_faces(S_SH + c, sh.at[c], (4, 2, 0))
        send_edges(S_SH + c, E_SH + c, -1)

    drain(*range(S_ONE, S_ONE + 3), *range(S_TWO, S_TWO + 3), S_VEL, S_DE)
    receive(S_DE, de)
    fields = (rho_f, de)
    wide = pl.ds(8, 40)
    wide_last = lax.broadcasted_iota(jnp.int32, (40, LANES), 1) == LANES - 1

    def receive_shift(c):
        wait_faces(S_SH + c, sh.at[c], (4, 2, 0))
        wait_edges(S_SH + c, E_SH + c, -1)
        edge_halo(S_SH + c, E_SH + c, sh.at[c], -1)
        return rows_up(E_SH + c)

    zx = receive_shift(0)
    z_ax = zx[0] + zx[1]

    def flux_x(i):
        a = [sh[0, h, i, ROWS, :] + sh[0, h, i, ABOVE, :] for h in range(2)]
        up = z_above(a[0], a[1], to_last(z_ax, i))
        out = []
        for h in range(2):
            s = 0.25 * (a[h] + up[h])
            for field in fields:
                out.append(s * jnp.where(s > 0, field[h, i, ROWS, :], field[h, i - 1, ROWS, :]))
        return tuple(out)

    def remap_x(k, before):
        for j in range(4):
            x = 4 * k + j
            now = flux_x(x + 2)
            for h in range(2):
                for f, field in enumerate(fields):
                    partial[f, h, x] = field[h, x + 1, ROWS, :] + (now[2 * h + f] - before[2 * h + f])
            before = now
        return before
    lax.fori_loop(0, N // 4, remap_x, flux_x(1))

    receive_shift(1)
    z_y = ze[E_SH + 1, wide, :]
    z_y = z_y + pltpu.roll(z_y, LANES - 2, 1)

    def remap_y(xs, carry):
        for j, x in enumerate(xs):
            i = x + 1
            t = [sh[1, h, i, wide, :] + sh[1, h, i + 1, wide, :] for h in range(2)]
            ra, rb = [pltpu.roll(v, LANES - 1, 1) for v in t]
            up = (jnp.where(wide_last, rb, ra), jnp.where(wide_last, to_last(z_y, i), rb))
            for h in range(2):
                s = 0.25 * (t[h] + up[h])
                for f, field in enumerate(fields):
                    gy[j, f, h] = s * jnp.where(s > 0, field[h, i, wide, :], field[h, i, pl.ds(7, 40), :])
        for j, x in enumerate(xs):
            for h in range(2):
                for f in range(2):
                    partial[f, h, x] = partial[f, h, x] + (gy[j, f, h, 1:N + 1, :] - gy[j, f, h, 0:N, :])
        return carry
    planes(remap_y, 0, 4)

    zz3 = receive_shift(2)
    z_z = zz3[0] + zz3[1]
    z_z = 0.25 * (z_z + pltpu.roll(z_z, LANES - 2, 1))
    for f, slot in enumerate((S_RHO, S_DE)):
        tab[f] = jnp.where(
            odd, z_halo(slot, 0), z_z * jnp.where(z_z > 0, z_halo(slot, 1), zs[slot]))

    for copy in along + across:
        copy.wait_send()
    drain(*sent)


def remap(
    vel, acc, relaxed, sh, de, rho_f, tab, partial,
    v_out, a_out, r_out, d_out, e_out,
    nr, out_sem,
):
    fields = (rho_f, de)
    outs = []

    def halves(k):
        return pl.ds(k * LANES, LANES)

    def write(src, dst, i, h):
        copy = pltpu.make_async_copy(src, dst, out_sem.at[i, h])
        copy.start()
        outs.append(copy)

    for c in range(3):
        for h in range(2):
            write(acc.at[c, h], a_out.at[c, :, :, halves(h)], c, h)
            write(vel.at[c, h, pl.ds(1, N), ROWS, :], v_out.at[c, :, :, halves(h)], 3 + c, h)
            write(relaxed.at[c, h], r_out.at[c, :, :, halves(h)], 6 + c, h)
    def remap_z(xs, carry):
        for x in xs:
            i = x + 1
            s = [
                0.25 * ((sh[2, h, i, ROWS, :] + sh[2, h, i, ABOVE, :])
                        + (sh[2, h, i + 1, ROWS, :] + sh[2, h, i + 1, ABOVE, :]))
                for h in range(2)
            ]
            for f, field in enumerate(fields):
                own = [field[h, i, ROWS, :] for h in range(2)]
                end = to_ends(tab[f], i)
                under = z_below(own[0], own[1], end)
                g = [s[h] * jnp.where(s[h] > 0, own[h], under[h]) for h in range(2)]
                over = z_above(g[0], g[1], end)
                for h in range(2):
                    nr[f, h, x] = partial[f, h, x] + (over[h] - g[h])
        return carry
    for part in range(4):
        lo = 8 * part
        planes(remap_z, 0, 4, lo, lo + 8)
        for f, out in enumerate((d_out, e_out)):
            for h in range(2):
                write(nr.at[f, h, pl.ds(lo, 8)], out.at[pl.ds(lo, 8), :, halves(h)], 9 + 4 * f + part, h)
    for copy in outs:
        copy.wait()


def solution(mesh):
    sizes = tuple(mesh.shape[name] for name in ("bx", "by", "bz"))
    vector = P(None, "bx", "by", "bz")
    scalar = P("bx", "by", "bz")

    def on_device(position, velocity, density, energy, pinned):
        def padded(*lead):
            return pltpu.VMEM(lead + (2, PX, PY, LANES), F32)

        def plain(*lead, dtype=F32):
            return pltpu.VMEM(lead + (2, N, N, LANES), dtype)

        dma = pltpu.SemaphoreType.DMA
        v3 = jax.ShapeDtypeStruct(position.shape, F32)
        v1 = jax.ShapeDtypeStruct(density.shape, F32)
        anywhere = pl.BlockSpec(memory_space=pl.ANY)

        def body(*refs):
            kernel(sizes, *refs)

        in_vmem = pl.BlockSpec(memory_space=pltpu.VMEM)
        handed = pl.pallas_call(
            body,
            name="lagrangian_step",
            out_shape=(
                padded(3), plain(3), plain(3), padded(3), padded(), padded(), pltpu.VMEM((2, N, LANES), F32),
                plain(2)),
            in_specs=[anywhere] * 5,
            out_specs=[in_vmem] * 8,
            scratch_shapes=[
                padded(), plain(), padded(3), padded(3), padded(3),
                plain(3), plain(3), plain(3), plain(dtype=jnp.int32), plain(), plain(),
                padded(3),
                pltpu.VMEM((SLOTS + 1, 2, 2, N, 1, LANES), F32),
                pltpu.VMEM((SLOTS + 1, 2, 2, N, 1, LANES), F32),
                pltpu.VMEM((SLOTS, N, LANES), F32),
                pltpu.VMEM((SLOTS, 2, N, LANES), F32),
                pltpu.VMEM((EDGES + 4, 2, 1, LANES), F32),
                pltpu.VMEM((EDGES, N, LANES), F32),
                pltpu.VMEM((EDGES, 8, LANES), F32),
                pltpu.VMEM((EDGES, 8, LANES), F32),
                pltpu.VMEM((EDGES, PY, LANES), F32),
                pltpu.VMEM((2 * LANES, 2 * LANES), jnp.bfloat16),
                pltpu.VMEM((4, 2, 2, 40, LANES), F32),
                pltpu.VMEM((24, LANES), F32),
                pltpu.VMEM((sizes[2] + 8, 1, LANES), F32),
                pltpu.VMEM((sizes[0] * sizes[1] + 8, 1, LANES), F32),
                dma((5, 2)),
                dma((SLOTS, 6)), dma((SLOTS, 6)), dma((EDGES, 4)), dma((EDGES, 4)),
                dma((sizes[2],)), dma((sizes[2],)),
                dma((sizes[0] * sizes[1],)), dma((sizes[0] * sizes[1],)),
            ],
            compiler_params=pltpu.CompilerParams(
                collective_id=0, has_side_effects=True, vmem_limit_bytes=43 * 1000 * 1000),
        )(position, velocity, density, energy, pinned)
        return tuple(pl.pallas_call(
            remap,
            name="remap",
            out_shape=(v3, v3, v3, v1, v1),
            in_specs=[in_vmem] * 8,
            out_specs=[anywhere] * 5,
            scratch_shapes=[plain(2), dma((17, 2))],
            compiler_params=pltpu.CompilerParams(vmem_limit_bytes=4 * 1000 * 1000),
        )(*handed))

    return jax.shard_map(
        on_device,
        mesh=mesh,
        in_specs=(vector, vector, scalar, scalar, scalar),
        out_specs=(vector, vector, vector, scalar, scalar),
        check_vma=False,
    )
```
